256 devices in a mesh: dom: 64 (over z, x, core), feat: 4 (over y).
Axes of the slice: x: 4, y: 4, z: 8, core: 2. Of those that a mesh axis runs over, the one named last changes fastest.
Arguments:
- features: float32 [98304, 1024], P('dom', 'feat'), may hold values from -6 to 6
- degree: int32 [98304], P('dom'), may hold values from 1 to 9
- diag_adj: float32 [98304, 128], P('dom'), may hold values from -0.25 to 0.25
- remote_adj: float32 [64, 48, 128, 128], P('dom'), may hold values from -0.25 to 0.25
- read_block: int32 [64, 64], P('dom'), may hold values from 0 to 12, as said below
- tile_src: int32 [64, 48], P('dom'), may hold values from 0 to 63, as said below
- tile_row: int32 [64, 48], P('dom'), may hold values from 0 to 11, as said below
- w_first: float32 [1024, 1024], P('feat'), may hold values from -0.25 to 0.25
- b_first: float32 [1024], replicated, may hold values from -2 to 2
- w_second: float32 [1024, 1024], P('feat'), may hold values from -0.25 to 0.25
- b_second: float32 [1024], replicated, may hold values from -2 to 2
Outputs:
- embed: float32 [98304, 1024], P(('dom', 'feat'))
The draws below stay inside these ranges and needn't reach their ends.
Inputs may be any that keep to these rules, and one draw needn't show every extreme that they name: `read_block`: entry [s, d] is the block of partition s that partition d reads, or 12 if d does not read s. Every partition reads exactly 24 other partitions, one block of each, and never itself. `tile_src`: tiles come in groups of 2 consecutive tiles with the same source partition; the sources of a partition's tiles are exactly the 24 partitions that it reads according to read_block. `tile_row`: within a group of 2 tiles with the same source, the block rows are distinct.
All inputs are finite; a program needn't handle non-finite values.
Results may differ from the reference program's by a relative error of at most 0.0003.
Values sent between devices are 32-bit elements; how exact they have to be, the bound alone decides.
A program may use at most 128 MiB of HBM per device.

```python
import jax
import jax.numpy as jnp
from jax import lax

HIDDEN_SIZE = 1024
TILE = 128
BLK_DEV = 12
TOUCH = 2
NPARTS = 64
READS = 24
REMOTE = 48
PART = 1536
VERTS = 98304


def graph_tables(key):
    base = jax.random.fold_in(key, 7)
    key_pop, key_noise, key_block, key_rows = jax.random.split(base, 4)
    popular = jax.random.randint(key_pop, (NPARTS,), 0, 4) * 256
    noise = jax.random.randint(key_noise, (NPARTS, NPARTS), 0, 1024)
    indices = jnp.arange(NPARTS, dtype=jnp.int32)
    score = (noise + popular[None, :]) * 4096 + indices[None, :]
    score = jnp.where(indices[:, None] == indices[None, :], -1, score)
    _, sources = lax.top_k(score, READS)
    sources = sources.astype(jnp.int32)
    chosen = jax.random.randint(key_block, (NPARTS, READS), 0, BLK_DEV)
    readers = jnp.broadcast_to(indices[:, None], sources.shape)
    table = jnp.full((NPARTS, NPARTS), BLK_DEV, jnp.int32).at[sources, readers].set(chosen.astype(jnp.int32))
    row_scores = jax.random.randint(key_rows, (NPARTS, READS, BLK_DEV), 0, 1 << 20) * BLK_DEV + jnp.arange(BLK_DEV, dtype=jnp.int32)
    _, rows = lax.top_k(row_scores, TOUCH)
    tile_rows = rows.astype(jnp.int32).reshape(NPARTS, REMOTE)
    tile_sources = jnp.broadcast_to(sources[:, :, None], (NPARTS, READS, TOUCH)).reshape(NPARTS, REMOTE)
    return (table, tile_sources, tile_rows)


def draw_read_block(key, part):
    return graph_tables(key)[0]


def draw_tile_src(key, part):
    return graph_tables(key)[1]


def draw_tile_row(key, part):
    return graph_tables(key)[2]


def with_ends(drawn, stream_key, smallest, top_value):
    spot = [jax.random.randint(jax.random.fold_in(stream_key, axis), (), 0, length) for axis, length in enumerate(drawn.shape)]
    longest = drawn.shape.index(max(drawn.shape))
    next_to = spot[:longest] + [(spot[longest] + 1) % drawn.shape[longest]] + spot[longest + 1:]
    return drawn.at[tuple(spot)].set(smallest).at[tuple(next_to)].set(top_value)


def level_of(key, shape, cuts, low, high):
    def one(dim, parts):
        steps = jax.random.uniform(jax.random.fold_in(jax.random.fold_in(key, 6), dim), (parts,), jnp.float32, low / len(cuts), high / len(cuts))
        return jnp.repeat(jnp.exp(steps), shape[dim] // parts).reshape((-1,) + (1,) * (len(shape) - dim - 1))

    level = one(*cuts[0])
    for cut in cuts[1:]:
        level = level * one(*cut)
    return level


def gaussian(rng, dims, scale, reach, cuts=(), kind=jnp.bfloat16):
    entries = jax.random.normal(rng, dims, jnp.float32) * scale
    if len(cuts) > 0:
        entries = level_of(rng, dims, cuts, -0.22, 0.18) * entries
    return jnp.clip(entries, min=-reach, max=reach).astype(kind)


def setup_inputs(seed: int = 0) -> dict:
    key_of = jax.random.split(jax.random.key(seed), 12)
    features = gaussian(key_of[0], (VERTS, HIDDEN_SIZE), 1.0, 6.0, ((0, 64), (1, 4)), jnp.float32)
    degree = with_ends(jax.random.randint(key_of[1], (VERTS,), 1, 10), jax.random.fold_in(key_of[1], 1), 1, 9).astype(jnp.int32)
    diag_adj = gaussian(key_of[2], (VERTS, TILE), (TILE * (1 + REMOTE // BLK_DEV)) ** -0.5, 0.25, ((0, 64),), jnp.float32)
    remote_adj = gaussian(key_of[3], (NPARTS, REMOTE, TILE, TILE), (TILE * (1 + REMOTE // BLK_DEV)) ** -0.5, 0.25, ((0, 64),), jnp.float32)
    read_block = draw_read_block(jax.random.fold_in(key_of[11], 71), 0)
    tile_src = draw_tile_src(jax.random.fold_in(key_of[11], 71), 0)
    tile_row = draw_tile_row(jax.random.fold_in(key_of[11], 71), 0)
    w_first = gaussian(key_of[7], (HIDDEN_SIZE, HIDDEN_SIZE), (HIDDEN_SIZE // 2) ** -0.5, 0.25, ((0, 4),), jnp.float32)
    b_first = gaussian(key_of[8], (HIDDEN_SIZE,), 0.3, 2.0, (), jnp.float32)
    w_second = gaussian(key_of[9], (HIDDEN_SIZE, HIDDEN_SIZE), (HIDDEN_SIZE // 2) ** -0.5, 0.25, ((0, 4),), jnp.float32)
    b_second = gaussian(key_of[10], (HIDDEN_SIZE,), 0.3, 2.0, (), jnp.float32)
    return dict(features=features, degree=degree, diag_adj=diag_adj, remote_adj=remote_adj, read_block=read_block, tile_src=tile_src, tile_row=tile_row, w_first=w_first, b_first=b_first, w_second=w_second, b_second=b_second)


def layer(hidden_in, scaling, diag_adj, remote_adj, read_block, tile_src, tile_row, weight, bias, rectify):
    width = hidden_in.shape[1]
    scaled = hidden_in * scaling[:, None]
    blocks = scaled.reshape(NPARTS, BLK_DEV, TILE, width)
    diag_tiles = diag_adj.reshape(NPARTS, BLK_DEV, TILE, TILE)
    part_scaling = scaling.reshape(NPARTS, PART)
    levels = jnp.arange(BLK_DEV, dtype=jnp.int32)

    def one_part(items):
        own_tiles, adjacency, sources, rows, part_index, row_scaling = items
        own_blocks = blocks[part_index]
        own = jnp.einsum('bij,bjf->bif', own_tiles, own_blocks, precision=lax.Precision.HIGHEST)
        chosen = read_block[sources, part_index]
        picked = blocks[sources, chosen]
        products = jnp.einsum('kij,kjf->kif', adjacency, picked, precision=lax.Precision.HIGHEST)
        row_onehot = (rows[None, :] == levels[:, None]).astype(scaled.dtype)
        remote = jnp.einsum('bk,kif->bif', row_onehot, products, precision=lax.Precision.HIGHEST)
        aggregated = (own + remote).reshape(PART, width) * row_scaling[:, None]
        mixed = jnp.dot(aggregated, weight, precision=lax.Precision.HIGHEST) + bias[None, :]
        if rectify:
            mixed = jnp.maximum(mixed, 0.0)
        return mixed
    result = lax.map(one_part, (diag_tiles, remote_adj, tile_src, tile_row, jnp.arange(NPARTS, dtype=jnp.int32), part_scaling))
    return result.reshape(VERTS, width)

def reference(features, degree, diag_adj, remote_adj, read_block, tile_src, tile_row, w_first, b_first, w_second, b_second):
    scaling = lax.rsqrt(degree.astype(jnp.float32))
    hidden = layer(features, scaling, diag_adj, remote_adj, read_block, tile_src, tile_row, w_first, b_first, True)
    return layer(hidden, scaling, diag_adj, remote_adj, read_block, tile_src, tile_row, w_second, b_second, False)
```

```python
import functools

import jax
import jax.numpy as jnp
from jax import lax
from jax.experimental import pallas as pl
from jax.experimental.pallas import tpu as pltpu
from jax.sharding import PartitionSpec as P

MESH = pl.DeviceIdType.MESH
F32 = jnp.float32
BF16 = jnp.bfloat16

TILE = 128
BLK = 12
REMOTE = 48
NZ, NX, NC, NY = 8, 4, 2, 4
PLANE = NX * NC
NPARTS = NZ * PLANE
HALF = 128
ROWS = BLK * TILE // NY
READERS = [(1, 0), (3, 0), (1, 1), (3, 1), (2, 0), (2, 1), (0, 1)]


def split(a):
    hi = a.astype(BF16)
    return hi, (a - hi.astype(F32)).astype(BF16)


def dot3(a, b):
    ah, al = split(a)
    bh, bl = split(b)
    out = jnp.dot(ah, bh, preferred_element_type=F32)
    out = out + jnp.dot(ah, bl, preferred_element_type=F32)
    return out + jnp.dot(al, bh, preferred_element_type=F32)


def layer_kernel(
    last_layer,
    tab,
    rbrow,
    feat,
    adj,
    diag,
    scal,
    weight,
    bias,
    out,
    zb00, zb01, zb02, zb10, zb11, zb12,
    zc00, zc01, zc02, zc10, zc11, zc12,
    zfar0, zfar1,
    inc0, inc1,
    sendbuf,
    runs,
    agg0, agg1,
    vert0, vert1,
    wg0, wg1,
    total,
    hid,
    tblv,
    tbls,
    sem_tsend, sem_trecv, sem_tloc,
    sem_zsend, sem_zrecv,
    sem_xsend, sem_xrecv,
    sem_wsend, sem_wrecv,
    sem_ysend, sem_yrecv,
    sem_bsend, sem_brecv,
):
    me = lax.axis_index("dom")
    y = lax.axis_index("feat")
    z = me // PLANE
    xc = lax.rem(me, PLANE)
    x = xc // NC
    c = lax.rem(xc, NC)
    zb = (((zb00, zb01, zb02), (zb10, zb11, zb12)), ((zc00, zc01, zc02), (zc10, zc11, zc12)))
    zfar = (zfar0, zfar1)
    inc = (inc0, inc1)
    agg = (agg0, agg1)
    vert = (vert0, vert1)
    wg = (wg0, wg1)

    def zpeer(step):
        return (lax.rem(z + (step + NZ), NZ) * PLANE + xc, y)

    def reader(dx, dc):
        return lax.rem(x + dx, NX) * NC + lax.rem(c + dc, NC)

    def ypeer(step):
        return lax.rem(y + step, NY)

    barrier = pltpu.get_barrier_semaphore()
    for dz in range(1, NZ):
        pl.semaphore_signal(barrier, inc=1, device_id=zpeer(dz), device_id_type=MESH)
    for dx, dc in READERS:
        pl.semaphore_signal(barrier, inc=1, device_id=(z * PLANE + reader(dx, dc), y), device_id_type=MESH)
    for dy in range(1, NY):
        pl.semaphore_signal(barrier, inc=1, device_id=(me, ypeer(dy)), device_id_type=MESH)
    pl.semaphore_wait(barrier, NZ - 1 + len(READERS) + NY - 1)

    def rdma(src, dst, send, recv, device):
        return pltpu.make_async_remote_copy(
            src_ref=src, dst_ref=dst, send_sem=send, recv_sem=recv, device_id=device, device_id_type=MESH
        )

    table_copies = [
        rdma(rbrow, tblv.at[dz], sem_tsend.at[dz], sem_trecv.at[dz], zpeer(dz)) for dz in range(1, NZ)
    ]
    for copy in table_copies:
        copy.start()
    own_table = pltpu.make_async_copy(rbrow, tbls.at[0], sem_tloc.at[0])
    own_table.start()

    def sub(ref, s):
        return ref.at[pl.ds(s * (BLK // 2), BLK // 2)]

    def own_sub(h, s):
        return feat.at[pl.ds(s * (BLK // 2), BLK // 2), :, pl.ds(h * HALF, HALF)]

    def zbuffer(h, way, d):
        return zfar[h] if d == NZ // 2 else zb[h][way][d - 1]

    def zcopy(h, way, d, s):
        src = own_sub(h, s) if d == 1 else sub(zbuffer(h, way, d - 1), s)
        return rdma(
            src,
            sub(zbuffer(h, way, d), s),
            sem_zsend.at[h, way, d - 1, s],
            sem_zrecv.at[h, way, d - 1, s],
            zpeer(1 if way == 0 else -1),
        )

    def start_own(h):
        for k in range(2):
            for way in range(2):
                zcopy(h, way, 1, k ^ way).start()

    started = []

    def weight_copy(h, dy):
        rows = pl.ds(y * HALF, HALF)
        return rdma(
            weight.at[pl.ds(h * HALF, HALF)],
            wg[h].at[rows],
            sem_wsend.at[h, dy - 1],
            sem_wrecv.at[h, dy - 1],
            (me, ypeer(dy)),
        )

    def serve(h, dz, order, load):
        zs = lax.rem(z + (dz + NZ), NZ)
        slot = zs * PLANE + xc
        entry = (-dz) % NZ
        base = (h * NZ + order) * len(READERS)
        for r, (dx, dc) in enumerate(READERS):
            want = tbls[entry, 0, z * PLANE + reader(dx, dc)]
            sendbuf[base + r] = load(jnp.minimum(want, BLK - 1))
        want = tbls[entry, 0, me]
        inc[h][slot] = load(jnp.minimum(want, BLK - 1))
        for r, (dx, dc) in enumerate(READERS):
            rdma(
                sendbuf.at[base + r],
                inc[h].at[slot],
                sem_xsend.at[h],
                sem_xrecv.at[h],
                (z * PLANE + reader(dx, dc), y),
            ).start()

    def serve_own(h):
        serve(h, 0, 0, lambda b: feat[b, :, h * HALF : (h + 1) * HALF])

    def serve_buffer(h, dz, order, ref):
        serve(h, dz, order, lambda b: ref[b])

    def wait_table(dz):
        table_copies[dz - 1].wait_recv()
        copy = pltpu.make_async_copy(tblv.at[dz], tbls.at[dz], sem_tloc.at[dz])
        copy.start()
        copy.wait()

    def distance(h, d):
        for k in range(2):
            for way in range(2):
                s = k ^ way
                zcopy(h, way, d, s).wait_recv()
                if d < NZ // 2 - 1 or k == 0:
                    zcopy(h, way, d + 1, s).start()
        if h == 0 and d == NZ // 2 - 1:
            start_own(1)
        for way in range(2):
            dz = -d if way == 0 else d
            if h == 0:
                wait_table(-dz % NZ)
            serve_buffer(h, dz, 2 * d - 1 + way, zbuffer(h, way, d))

    def farthest(h):
        d = NZ // 2
        for way in range(2):
            zcopy(h, way, d, way).wait_recv()
        if h == 0:
            wait_table(d)
        serve_buffer(h, d, NZ - 1, zfar[h])

    def ycopy(h, dy):
        n = ypeer(dy)
        return rdma(
            agg[h].at[pl.ds(n * ROWS, ROWS)],
            vert[h].at[:, pl.ds(pl.multiple_of(y * HALF, HALF), HALF)],
            sem_ysend.at[h, dy - 1],
            sem_yrecv.at[h, dy - 1],
            (me, n),
        )

    def aggregate(h):
        many = NPARTS - NZ
        pltpu.make_async_copy(inc[h].at[pl.ds(0, many)], inc[h].at[pl.ds(0, many)], sem_xrecv.at[h]).wait()

        def step(p, acc):
            product = dot3(adj[tab[0, p]], inc[h][tab[1, p]])
            acc = acc * tab[2, p].astype(F32) + product
            runs[p] = acc
            return acc

        lax.fori_loop(0, REMOTE, step, jnp.zeros((TILE, HALF), F32))
        runs[REMOTE] = jnp.zeros((TILE, HALF), F32)
        for dy in (1, 2, 3, 0):
            n = ypeer(dy)

            def finish(j, carry):
                i = n * (BLK // NY) + j
                own = dot3(diag[i], feat[i, :, h * HALF : (h + 1) * HALF])
                value = (own + runs[tab[3, i]]) * scal[i]
                if dy:
                    agg[h][pl.ds(pl.multiple_of(i * TILE, TILE), TILE), :] = value
                else:
                    vert[h][pl.ds(pl.multiple_of(j * TILE, TILE), TILE), pl.ds(pl.multiple_of(y * HALF, HALF), HALF)] = value
                return carry

            lax.fori_loop(0, BLK // NY, finish, 0)
            if dy:
                ycopy(h, dy).start()

    def wait_inputs(h):
        for dy in range(1, NY):
            ycopy(h, dy).wait_recv()
            weight_copy(h, dy).wait_recv()

    def columns(n):
        return pl.ds(pl.multiple_of(n * 256, 256), 256)

    def first_product():
        wait_inputs(0)

        def step(n, carry):
            total[n] = dot3(vert[0][...], wg[0][:, columns(n)]) + bias[:, columns(n)]
            return carry

        lax.fori_loop(0, NY, step, 0)

    def back(n, k):
        return rdma(
            hid.at[n], out.at[pl.ds(y * ROWS, ROWS)], sem_bsend.at[k], sem_brecv.at[k], (me, n)
        )

    def second_product():
        wait_inputs(1)

        def value(n):
            return total[n] + dot3(vert[1][...], wg[1][:, columns(n)])

        if last_layer:

            def step(n, carry):
                out[:, columns(n)] = value(n)
                return carry

            lax.fori_loop(0, NY, step, 0)
            return
        factor = scal[pl.ds(y * (BLK // NY), BLK // NY)].reshape(ROWS, HALF)

        def hidden(n):
            return jnp.maximum(value(n), 0.0) * jnp.concatenate([factor, factor], axis=1)

        def step(k, carry):
            n = ypeer(k + 1)
            hid[n] = hidden(n)
            back(n, k).start()
            return carry

        lax.fori_loop(0, NY - 1, step, 0)
        out[pl.ds(pl.multiple_of(y * ROWS, ROWS), ROWS), :] = hidden(y)
        for k in range(NY - 1):
            back(ypeer(k + 1), k).wait()

    start_own(0)
    for h in range(2):
        for dy in range(1, NY):
            weight_copy(h, dy).start()
    own_table.wait()
    for h in range(2):
        wg[h][pl.ds(pl.multiple_of(y * HALF, HALF), HALF), :] = weight[pl.ds(h * HALF, HALF), :]
    serve_own(0)
    for d in range(1, NZ // 2):
        distance(0, d)
    farthest(0)
    serve_own(1)
    distance(1, 1)
    aggregate(0)
    distance(1, 2)
    first_product()
    distance(1, 3)
    farthest(1)
    aggregate(1)
    second_product()

    for copy in table_copies:
        copy.wait_send()
    for h in range(2):
        for way in range(2):
            for d in range(1, NZ // 2 + 1):
                for s in range(2):
                    if d < NZ // 2 or s == way:
                        zcopy(h, way, d, s).wait_send()
        for dy in range(1, NY):
            weight_copy(h, dy).wait_send()
            ycopy(h, dy).wait_send()
        many = pl.ds(h * NZ * len(READERS), NZ * len(READERS))
        pltpu.make_async_copy(sendbuf.at[many], sendbuf.at[many], sem_xsend.at[h]).wait()


def layer(last_layer, tab, rbrow, feat, adj, diag, scal, weight, bias):
    vmem = pl.BlockSpec(memory_space=pltpu.VMEM)
    smem = pl.BlockSpec(memory_space=pltpu.SMEM)
    dma = pltpu.SemaphoreType.DMA
    chunk = pltpu.VMEM((BLK, TILE, HALF), F32)
    shape = (ROWS, NY * 256) if last_layer else (NY * ROWS, 256)
    return pl.pallas_call(
        functools.partial(layer_kernel, last_layer),
        name="layer_two" if last_layer else "layer_one",
        out_shape=jax.ShapeDtypeStruct(shape, F32),
        in_specs=[smem] + [vmem] * 7,
        out_specs=vmem,
        scratch_shapes=[chunk] * 14
        + [pltpu.VMEM((NPARTS, TILE, HALF), F32)] * 2
        + [
            pltpu.VMEM((2 * NZ * len(READERS), TILE, HALF), F32),
            pltpu.VMEM((REMOTE + 1, TILE, HALF), F32),
        ]
        + [pltpu.VMEM((NY * ROWS, HALF), F32)] * 2
        + [pltpu.VMEM((ROWS, NY * HALF), F32)] * 2
        + [pltpu.VMEM((NY * HALF, 4 * 256), F32)] * 2
        + [
            pltpu.VMEM((NY, ROWS, 256), F32),
            pltpu.VMEM((NY, ROWS, 256), F32),
            pltpu.VMEM((NZ, 8, 128), jnp.int32),
            pltpu.SMEM((NZ, 8, 128), jnp.int32),
            dma((NZ,)),
            dma((NZ,)),
            dma((NZ,)),
            dma((2, 2, 4, 2)),
            dma((2, 2, 4, 2)),
            dma((2,)),
            dma((2,)),
            dma((2, 3)),
            dma((2, 3)),
            dma((2, 3)),
            dma((2, 3)),
            dma((3,)),
            dma((3,)),
        ],
        compiler_params=pltpu.CompilerParams(
            collective_id=int(last_layer), has_side_effects=True, vmem_limit_bytes=63 * 1024 * 1024
        ),
    )(tab, rbrow, feat, adj, diag, scal, weight, bias)


def tile_order(tile_src, tile_row):
    k = jnp.arange(REMOTE, dtype=jnp.int32)
    key = tile_row * REMOTE + k
    rank = jnp.sum((key[None, :] < key[:, None]).astype(jnp.int32), axis=1)
    place = (rank[None, :] == k[:, None]).astype(jnp.int32)
    perm = jnp.sum(place * k[None, :], axis=1)
    source = jnp.sum(place * tile_src[None, :], axis=1)
    row = jnp.sum(place * tile_row[None, :], axis=1)
    same = jnp.concatenate([jnp.zeros((1,), jnp.int32), (row[1:] == row[:-1]).astype(jnp.int32)])
    levels = jnp.arange(BLK, dtype=jnp.int32)
    upto = jnp.sum((tile_row[None, :] <= levels[:, None]).astype(jnp.int32), axis=1)
    here = jnp.sum((tile_row[None, :] == levels[:, None]).astype(jnp.int32), axis=1)
    last = jnp.where(here > 0, upto - 1, REMOTE)
    return jnp.stack([perm, source, same, jnp.pad(last, (0, REMOTE - BLK))])


def per_device(
    features, degree, diag_adj, remote_adj, read_block, tile_src, tile_row, w_first, b_first, w_second, b_second
):
    scaling = lax.rsqrt(degree.astype(F32))
    scaled = features * scaling[:, None]
    scal = jnp.broadcast_to(scaling[:, None], (BLK * TILE, TILE)).reshape(BLK, TILE, TILE)
    tab = tile_order(tile_src[0], tile_row[0])
    rbrow = jnp.zeros((8, 128), jnp.int32).at[0, :NPARTS].set(read_block[0])
    diag = diag_adj.reshape(BLK, TILE, TILE)
    shared = (remote_adj[0], diag, scal)
    hidden = layer(False, tab, rbrow, scaled.reshape(BLK, TILE, 256), *shared, w_first, b_first[None, :])
    return layer(True, tab, rbrow, hidden.reshape(BLK, TILE, 256), *shared, w_second, b_second[None, :])


def solution(mesh):
    return jax.shard_map(
        per_device,
        mesh=mesh,
        in_specs=(
            P("dom", "feat"),
            P("dom"),
            P("dom", None),
            P("dom", None, None, None),
            P("dom", None),
            P("dom", None),
            P("dom", None),
            P("feat", None),
            P(),
            P("feat", None),
            P(),
        ),
        out_specs=P(("dom", "feat"), None),
        check_vma=False,
    )
```

```python
import functools

import jax
import jax.numpy as jnp
from jax import lax
from jax.experimental import pallas as pl
from jax.experimental.pallas import tpu as pltpu
from jax.sharding import PartitionSpec as P

MESH = pl.DeviceIdType.MESH
F32 = jnp.float32
BF16 = jnp.bfloat16

TILE = 128
BLK = 12
REMOTE = 48
GROUPS = 24
NZ, NX, NC, NY = 8, 4, 2, 4
PLANE = NX * NC
NPARTS = NZ * PLANE
HALF = 128
FEAT = 2 * HALF
SUBS = 2
SUBROWS = TILE // SUBS
NEAR = NZ // 2 - 1
MINE = BLK // NY
ROWS = MINE * TILE
READERS = [(1, 0), (3, 0), (1, 1), (3, 1), (2, 0), (2, 1), (0, 1)]
NREAD = len(READERS)
TABLE_STEPS = [1, 2, 3, NZ - 3, NZ - 2, NZ - 1]
SENDS = SUBS * (NREAD + 2 * (NEAR - 1) * NREAD + 2 * (NREAD + NX))
ARRIVALS = (NZ - 1) * NREAD + PLANE


def split(a):
    hi = a.astype(BF16)
    return hi, (a - hi.astype(F32)).astype(BF16)


def dot3s(ah, al, bh, bl):
    out = jnp.dot(ah, bh, preferred_element_type=F32)
    out = out + jnp.dot(ah, bl, preferred_element_type=F32)
    return out + jnp.dot(al, bh, preferred_element_type=F32)


def dot3(a, b):
    return dot3s(*split(a), *split(b))


def both_layers(*refs):
    refs = list(refs)

    def take(n):
        got = refs[:n]
        del refs[:n]
        return got

    tab, rbrow, degree, raw, adj_hbm, diag, w1, b1, w2, b2, out = take(11)
    zflat = take(2 * 2 * NEAR * SUBS)
    zbuf = [
        [[[zflat[((h * 2 + way) * NEAR + d) * SUBS + s] for s in range(SUBS)] for d in range(NEAR)] for way in range(2)]
        for h in range(2)
    ]
    inc = take(2)
    sendbuf, prod, runs, adjhi, adjlo = take(5)
    agg = take(2)
    vertflat = take(4)
    vert = [vertflat[:2], vertflat[2:]]
    wgflat = take(4)
    wg = [wgflat[:2], wgflat[2:]]
    total, hid = take(2)
    featflat = take(4)
    feats = [featflat[:2], featflat[2:]]
    scal, tblv, tbls = take(3)
    weights = [w1, w2]
    biases = [b1, b2]
    sem_tsend, sem_trecv, sem_tloc, sem_zsend, sem_zrecv, sem_xsend, sem_xrecv = take(7)
    sem_wsend, sem_wrecv, sem_wloc, sem_ysend, sem_yrecv, sem_bsend, sem_brecv, sem_adj, free = take(9)

    me = lax.axis_index("dom")
    y = lax.axis_index("feat")
    z = me // PLANE
    xc = lax.rem(me, PLANE)
    x = xc // NC
    c = lax.rem(xc, NC)

    def plane(step):
        return lax.rem(z + (step + NZ), NZ) * PLANE

    def seat(dx, dc):
        return lax.rem(x + dx, NX) * NC + lax.rem(c + dc, NC)

    def ypeer(step):
        return lax.rem(y + step, NY)

    def rdma(src, dst, send, recv, device):
        return pltpu.make_async_remote_copy(
            src_ref=src, dst_ref=dst, send_sem=send, recv_sem=recv, device_id=device, device_id_type=MESH
        )

    def signal(sem, device):
        pl.semaphore_signal(sem, inc=1, device_id=device, device_id_type=MESH)

    def signal_writers(sem):
        for step in (1, -1):
            signal(sem, (plane(step) + xc, y))
        for dx, dc in READERS:
            signal(sem, (plane(0) + seat(dx, dc), y))
        beyond = lax.rem(z + (2 * c - 1 + NZ), NZ) * PLANE
        for j in range(PLANE):
            signal(sem, (beyond + j, y))

    writers = 2 + NREAD + PLANE

    adj_copy = pltpu.make_async_copy(adj_hbm, prod, sem_adj)
    adj_copy.start()
    own_weights = []
    for l in range(2):
        for h in range(2):
            own_weights.append(
                pltpu.make_async_copy(
                    weights[l].at[pl.ds(h * HALF, HALF)],
                    wg[l][h].at[pl.ds(pl.multiple_of(y * HALF, HALF), HALF)],
                    sem_wloc.at[l, h],
                )
            )
    for copy in own_weights:
        copy.start()
    own_table = pltpu.make_async_copy(rbrow, tbls.at[0], sem_tloc.at[0])
    own_table.start()

    barrier = pltpu.get_barrier_semaphore()
    for dz in TABLE_STEPS[1:-1]:
        signal(barrier, (plane(dz) + xc, y))
    for dy in range(1, NY):
        signal(barrier, (me, ypeer(dy)))
    signal_writers(barrier)

    def scale(i, carry):
        row = lax.rsqrt(degree[pl.ds(i, 1), :].astype(F32))
        scal[i] = jnp.transpose(jnp.broadcast_to(row, (TILE, TILE)))
        factor = scal[i]
        for h in range(2):
            feats[0][h][i] = raw[i, :, h * HALF : (h + 1) * HALF] * factor
        return carry

    lax.fori_loop(0, BLK, scale, 0)
    pl.semaphore_wait(barrier, len(TABLE_STEPS) - 2 + NY - 1 + writers)

    table_copies = {
        dz: rdma(rbrow, tblv.at[dz], sem_tsend.at[dz], sem_trecv.at[dz], (plane(dz) + xc, y)) for dz in TABLE_STEPS
    }

    def wait_table(dz):
        table_copies[dz].wait_recv()
        copy = pltpu.make_async_copy(tblv.at[dz], tbls.at[dz], sem_tloc.at[dz])
        copy.start()
        copy.wait()

    def weight_copy(l, h, dy):
        return rdma(
            weights[l].at[pl.ds(h * HALF, HALF)],
            wg[l][h].at[pl.ds(pl.multiple_of(y * HALF, HALF), HALF)],
            sem_wsend.at[l, h, dy - 1],
            sem_wrecv.at[l, h, dy - 1],
            (me, ypeer(dy)),
        )

    def columns(n):
        return pl.ds(pl.multiple_of(n * FEAT, FEAT), FEAT)

    def run_layer(l):
        feat = feats[l]

        def zcopy(h, way, d, s):
            if d == 1:
                src = feat[h].at[:, pl.ds(s * SUBROWS, SUBROWS)]
            else:
                src = zbuf[h][way][d - 2][s]
            return rdma(
                src,
                zbuf[h][way][d - 1][s],
                sem_zsend.at[h, way, d - 1, s],
                sem_zrecv.at[h, way, d - 1, s],
                (plane(1 if way == 0 else -1) + xc, y),
            )

        def start_own(h):
            for s in range(SUBS):
                for way in range(2):
                    zcopy(h, way, 1, s).start()

        position = [0, 0]

        def serve(h, dz, s, load, beyond=None):
            slot = plane(dz) + xc
            entry = (-dz) % NZ
            rows = pl.ds(s * SUBROWS, SUBROWS)
            targets = []
            if beyond is not None:
                targets = [plane(beyond) + lax.rem(x + dx, NX) * NC + (0 if beyond == 1 else 1) for dx in range(NX)]
            targets = targets + [plane(0) + seat(dx, dc) for dx, dc in READERS]
            base = position[h]
            position[h] += len(targets)
            for r, target in enumerate(targets):
                sendbuf[h * SENDS + base + r] = load(jnp.minimum(tbls[entry, 0, target], BLK - 1))
            inc[h][slot, rows, :] = load(jnp.minimum(tbls[entry, 0, me], BLK - 1))
            for r, target in enumerate(targets):
                rdma(
                    sendbuf.at[h * SENDS + base + r],
                    inc[h].at[slot, rows],
                    sem_xsend.at[h],
                    sem_xrecv.at[h],
                    (target, y),
                ).start()

        def serve_own(h):
            for s in range(SUBS):
                serve(h, 0, s, lambda b: feat[h][b, s * SUBROWS : (s + 1) * SUBROWS, :])

        def distance(h, d):
            for s in range(SUBS):
                for way in range(2):
                    zcopy(h, way, d, s).wait_recv()
                    if d < NEAR:
                        zcopy(h, way, d + 1, s).start()
                if h == 0 and d == NEAR - 1 and s == SUBS - 1:
                    if l == 1:
                        wait_back(1)
                    start_own(1)
                for way in range(2):
                    dz = -d if way == 0 else d
                    if l == 0 and h == 0 and s == 0:
                        wait_table(-dz % NZ)
                    ref = zbuf[h][way][d - 1][s]
                    beyond = None
                    if d == NEAR:
                        beyond = 1 if way == 0 else -1
                    serve(h, dz, s, lambda b: ref[b], beyond)

        def ycopy(h, dy):
            n = ypeer(dy)
            return rdma(
                agg[h].at[pl.ds(pl.multiple_of(n * ROWS, ROWS), ROWS)],
                vert[l][h].at[:, pl.ds(pl.multiple_of(y * HALF, HALF), HALF)],
                sem_ysend.at[h, dy - 1],
                sem_yrecv.at[h, dy - 1],
                (me, n),
            )

        def own_tiles(h):
            def step(i, carry):
                agg[h][pl.ds(pl.multiple_of(i * TILE, TILE), TILE), :] = dot3(
                    diag[i], feat[h][i]
                )
                return carry

            lax.fori_loop(0, BLK, step, 0, unroll=2)

        def aggregate(h):
            many = inc[h].at[pl.ds(0, ARRIVALS)]
            pltpu.make_async_copy(many, many, sem_xrecv.at[h]).wait()

            def group(g, carry):
                block_hi, block_lo = split(inc[h][tab[3, g]])
                pair = dot3s(adjhi[g], adjlo[g], block_hi, block_lo)
                prod[2 * g] = pair[:TILE]
                prod[2 * g + 1] = pair[TILE:]
                return carry

            lax.fori_loop(0, GROUPS, group, 0, unroll=4)

            def run(p, acc):
                acc = acc * tab[1, p].astype(F32) + prod[tab[0, p]]
                runs[p] = acc
                return acc

            lax.fori_loop(0, REMOTE, run, jnp.zeros((TILE, HALF), F32), unroll=4)
            for dy in (1, 2, 3, 0):
                n = ypeer(dy)
                for j in range(MINE):
                    i = n * MINE + j
                    rows = pl.ds(pl.multiple_of(i * TILE, TILE), TILE)
                    value = (agg[h][rows, :] + runs[tab[2, i]]) * scal[i]
                    if dy:
                        agg[h][rows, :] = value
                    else:
                        vert[l][h][j * TILE : (j + 1) * TILE, pl.ds(pl.multiple_of(y * HALF, HALF), HALF)] = value
                if dy:
                    ycopy(h, dy).start()

        def wait_inputs(h):
            own_weights[l * 2 + h].wait()
            for dy in range(1, NY):
                weight_copy(l, h, dy).wait_recv()
            for dy in range(1, NY):
                ycopy(h, dy).wait_recv()

        def first_product():
            wait_inputs(0)

            def step(n, carry):
                total[n] = dot3(vert[l][0][...], wg[l][0][:, columns(n)]) + biases[l][:, columns(n)]
                return carry

            lax.fori_loop(0, NY, step, 0)

        def value(n):
            return total[n] + dot3(vert[l][1][...], wg[l][1][:, columns(n)])

        def last_product():
            wait_inputs(1)

            def step(n, carry):
                out[:, columns(n)] = value(n)
                return carry

            lax.fori_loop(0, NY, step, 0)

        def hidden_product():
            wait_inputs(1)
            factor = scal[pl.ds(y * MINE, MINE)]

            def hidden(n):
                found = jnp.maximum(value(n), 0.0).reshape(MINE, TILE, FEAT)
                return found * jnp.concatenate([factor, factor], axis=2)

            def step(k, carry):
                n = ypeer(k + 1)
                hid[n] = hidden(n)
                back(0, k).start()
                return carry

            lax.fori_loop(0, NY - 1, step, 0)
            for k in range(NY - 1):
                back(1, k).start()
            mine = hidden(y)
            for h in range(2):
                feats[1][h][pl.ds(y * MINE, MINE)] = mine[:, :, h * HALF : (h + 1) * HALF]

        def finish_sends():
            for h in range(2):
                for way in range(2):
                    for d in range(1, NEAR + 1):
                        for s in range(SUBS):
                            zcopy(h, way, d, s).wait_send()
                many = sendbuf.at[pl.ds(h * SENDS, SENDS)]
                pltpu.make_async_copy(many, many, sem_xsend.at[h]).wait()

        def finish_exchange():
            for h in range(2):
                for dy in range(1, NY):
                    ycopy(h, dy).wait_send()
                    weight_copy(l, h, dy).wait_send()

        if l == 1:
            wait_back(0)
            pl.semaphore_wait(free, writers)
        start_own(0)
        if l == 0:
            for copy in table_copies.values():
                copy.start()
            for ll in range(2):
                for h in range(2):
                    for dy in range(1, NY):
                        weight_copy(ll, h, dy).start()
            own_table.wait()
        serve_own(0)
        if l == 0:
            adj_copy.wait()

            def presplit(g, carry):
                for t in range(2):
                    hi, lo = split(prod[2 * g + t])
                    adjhi[g, t * TILE : (t + 1) * TILE, :] = hi
                    adjlo[g, t * TILE : (t + 1) * TILE, :] = lo
                return carry

            lax.fori_loop(0, GROUPS, presplit, 0)
            runs[REMOTE] = jnp.zeros((TILE, HALF), F32)
        own_tiles(0)
        distance(0, 1)
        distance(0, 2)
        distance(0, 3)
        serve_own(1)
        distance(1, 1)
        aggregate(0)
        own_tiles(1)
        distance(1, 2)
        first_product()
        distance(1, 3)
        aggregate(1)
        finish_sends()
        if l == 0:
            signal_writers(free)
            hidden_product()
        else:
            last_product()
        finish_exchange()

    def back(h, k):
        n = ypeer(k + 1)
        cols = pl.ds(h * HALF, HALF)
        return rdma(
            hid.at[n, :, :, cols],
            feats[1][h].at[pl.ds(y * MINE, MINE)],
            sem_bsend.at[h, k],
            sem_brecv.at[h, k],
            (me, n),
        )

    def wait_back(h):
        for k in range(NY - 1):
            back(h, k).wait()

    run_layer(0)
    run_layer(1)
    for copy in table_copies.values():
        copy.wait_send()


def network(tab, rbrow, degree, features, adj, diag, w1, b1, w2, b2):
    vmem = pl.BlockSpec(memory_space=pltpu.VMEM)
    smem = pl.BlockSpec(memory_space=pltpu.SMEM)
    anyw = pl.BlockSpec(memory_space=pl.ANY)
    dma = pltpu.SemaphoreType.DMA
    return pl.pallas_call(
        both_layers,
        name="both_layers",
        out_shape=jax.ShapeDtypeStruct((ROWS, NY * FEAT), F32),
        in_specs=[smem, vmem, vmem, vmem, anyw, vmem, anyw, vmem, anyw, vmem],
        out_specs=vmem,
        scratch_shapes=[pltpu.VMEM((BLK, SUBROWS, HALF), F32)] * (2 * 2 * NEAR * SUBS)
        + [pltpu.VMEM((NPARTS, TILE, HALF), F32)] * 2
        + [
            pltpu.VMEM((2 * SENDS, SUBROWS, HALF), F32),
            pltpu.VMEM((REMOTE, TILE, HALF), F32),
            pltpu.VMEM((REMOTE + 1, TILE, HALF), F32),
            pltpu.VMEM((GROUPS, 2 * TILE, TILE), BF16),
            pltpu.VMEM((GROUPS, 2 * TILE, TILE), BF16),
        ]
        + [pltpu.VMEM((NY * ROWS, HALF), F32)] * 2
        + [pltpu.VMEM((ROWS, NY * HALF), F32)] * 4
        + [pltpu.VMEM((NY * HALF, NY * FEAT), F32)] * 4
        + [
            pltpu.VMEM((NY, ROWS, FEAT), F32),
            pltpu.VMEM((NY, MINE, TILE, FEAT), F32),
        ]
        + [pltpu.VMEM((BLK, TILE, HALF), F32)] * 4
        + [
            pltpu.VMEM((BLK, TILE, TILE), F32),
            pltpu.VMEM((NZ, 8, 128), jnp.int32),
            pltpu.SMEM((NZ, 8, 128), jnp.int32),
            dma((NZ,)),
            dma((NZ,)),
            dma((NZ,)),
            dma((2, 2, NEAR, SUBS)),
            dma((2, 2, NEAR, SUBS)),
            dma((2,)),
            dma((2,)),
            dma((2, 2, 3)),
            dma((2, 2, 3)),
            dma((2, 2)),
            dma((2, 3)),
            dma((2, 3)),
            dma((2, 3)),
            dma((2, 3)),
            dma,
            pltpu.SemaphoreType.REGULAR,
        ],
        compiler_params=pltpu.CompilerParams(
            collective_id=0, has_side_effects=True, vmem_limit_bytes=67_000_000
        ),
    )(tab, rbrow, degree, features, adj, diag, w1, b1, w2, b2)


def prepare_kernel(tile_src, tile_row, read_block, tab, rbrow, place):
    def clear(i, carry):
        place[i] = 0
        tab[2, i] = REMOTE
        return carry

    lax.fori_loop(0, BLK + 1, clear, 0)

    def count(k, carry):
        r = tile_row[0, k] + 1
        place[r] = place[r] + 1
        return carry

    lax.fori_loop(0, REMOTE, count, 0)

    def accumulate(i, carry):
        place[i] = place[i] + place[i - 1]
        return carry

    lax.fori_loop(1, BLK + 1, accumulate, 0)

    def put(k, carry):
        r = tile_row[0, k]
        p = place[r]
        tab[0, p] = k
        tab[1, p] = (tab[2, r] != REMOTE).astype(jnp.int32)
        tab[2, r] = p
        place[r] = p + 1
        return carry

    lax.fori_loop(0, REMOTE, put, 0)

    def source(g, carry):
        tab[3, g] = tile_src[0, 2 * g]
        return carry

    lax.fori_loop(0, GROUPS, source, 0)
    rbrow[0:1, 0:NPARTS] = read_block[...]


def prepare(tile_src, tile_row, read_block):
    vmem = pl.BlockSpec(memory_space=pltpu.VMEM)
    smem = pl.BlockSpec(memory_space=pltpu.SMEM)
    return pl.pallas_call(
        prepare_kernel,
        name="prepare",
        out_shape=(jax.ShapeDtypeStruct((4, 128), jnp.int32), jax.ShapeDtypeStruct((8, 128), jnp.int32)),
        in_specs=[smem, smem, vmem],
        out_specs=(smem, vmem),
        scratch_shapes=[pltpu.SMEM((BLK + 4,), jnp.int32)],
    )(tile_src, tile_row, read_block)


def per_device(
    features, degree, diag_adj, remote_adj, read_block, tile_src, tile_row, w_first, b_first, w_second, b_second
):
    tab, rbrow = prepare(tile_src, tile_row, read_block)
    return network(
        tab,
        rbrow,
        degree.reshape(BLK, TILE),
        features.reshape(BLK, TILE, FEAT),
        remote_adj[0],
        diag_adj.reshape(BLK, TILE, TILE),
        w_first,
        b_first[None, :],
        w_second,
        b_second[None, :],
    )


def solution(mesh):
    return jax.shard_map(
        per_device,
        mesh=mesh,
        in_specs=(
            P("dom", "feat"),
            P("dom"),
            P("dom", None),
            P("dom", None, None, None),
            P("dom", None),
            P("dom", None),
            P("dom", None),
            P("feat", None),
            P(),
            P("feat", None),
            P(),
        ),
        out_specs=P(("dom", "feat"), None),
        check_vma=False,
    )
```

```python
import functools

import jax
import jax.numpy as jnp
from jax import lax
from jax.experimental import pallas as pl
from jax.experimental.pallas import tpu as pltpu
from jax.sharding import PartitionSpec as P

MESH = pl.DeviceIdType.MESH
F32 = jnp.float32
BF16 = jnp.bfloat16

TILE = 128
BLK = 12
REMOTE = 48
GROUPS = 24
NZ, NX, NC, NY = 8, 4, 2, 4
PLANE = NX * NC
NPARTS = NZ * PLANE
HALF = 128
FEAT = 2 * HALF
NEAR = NZ // 2 - 2
MINE = BLK // NY
ROWS = MINE * TILE
READERS = [(1, 0), (3, 0), (1, 1), (3, 1), (2, 0), (2, 1), (0, 1)]
NREAD = len(READERS)
TABLE_STEPS = [1, 2, NZ - 2, NZ - 1]
SENDS = (1 + 2 * NEAR) * NREAD + 2 * (PLANE + NX)
ARRIVALS = (1 + 2 * NEAR) * NREAD + 2 * PLANE + PLANE


def split(a):
    hi = a.astype(BF16)
    return hi, (a - hi.astype(F32)).astype(BF16)


def dot3s(ah, al, bh, bl):
    out = jnp.dot(ah, bh, preferred_element_type=F32)
    out = out + jnp.dot(ah, bl, preferred_element_type=F32)
    return out + jnp.dot(al, bh, preferred_element_type=F32)


def dot3(a, b):
    return dot3s(*split(a), *split(b))


def both_layers(*refs):
    refs = list(refs)

    def take(n):
        got = refs[:n]
        del refs[:n]
        return got

    tab, rbrow, degree, raw, adj_hbm, diag, w1, b1, w2, b2, out = take(11)
    zflat = take(2 * 2 * NEAR)
    zbuf = [[[zflat[(h * 2 + way) * NEAR + d] for d in range(NEAR)] for way in range(2)] for h in range(2)]
    inc = take(2)
    sendbuf, prod, runs, adjhi, adjlo = take(5)
    agg = take(2)
    vertflat = take(4)
    vert = [vertflat[:2], vertflat[2:]]
    wgflat = take(4)
    wg = [wgflat[:2], wgflat[2:]]
    total, hid = take(2)
    featflat = take(4)
    feats = [featflat[:2], featflat[2:]]
    scal, tblv, tbls = take(3)
    weights = [w1, w2]
    biases = [b1, b2]
    sem_tsend, sem_trecv, sem_tloc, sem_zsend, sem_zrecv, sem_xsend, sem_xrecv = take(7)
    sem_wsend, sem_wrecv, sem_wloc, sem_ysend, sem_yrecv, sem_bsend, sem_brecv, sem_adj, free = take(9)

    me = lax.axis_index("dom")
    y = lax.axis_index("feat")
    z = me // PLANE
    xc = lax.rem(me, PLANE)
    x = xc // NC
    c = lax.rem(xc, NC)

    def plane(step):
        return lax.rem(z + (step + NZ), NZ) * PLANE

    def seat(dx, dc):
        return lax.rem(x + dx, NX) * NC + lax.rem(c + dc, NC)

    def ypeer(step):
        return lax.rem(y + step, NY)

    def rdma(src, dst, send, recv, device):
        return pltpu.make_async_remote_copy(
            src_ref=src, dst_ref=dst, send_sem=send, recv_sem=recv, device_id=device, device_id_type=MESH
        )

    def signal(sem, device):
        pl.semaphore_signal(sem, inc=1, device_id=device, device_id_type=MESH)

    def signal_writers(sem):
        for dx, dc in READERS:
            signal(sem, (plane(0) + seat(dx, dc), y))
        beyond = lax.rem(z + (4 * c - 2 + NZ), NZ) * PLANE
        for j in range(PLANE):
            signal(sem, (plane(1) + j, y))
            signal(sem, (plane(-1) + j, y))
            signal(sem, (beyond + j, y))

    writers = NREAD + 3 * PLANE

    adj_copy = pltpu.make_async_copy(adj_hbm, prod, sem_adj)
    adj_copy.start()
    own_weights = []
    for l in range(2):
        for h in range(2):
            own_weights.append(
                pltpu.make_async_copy(
                    weights[l].at[pl.ds(h * HALF, HALF)],
                    wg[l][h].at[pl.ds(pl.multiple_of(y * HALF, HALF), HALF)],
                    sem_wloc.at[l, h],
                )
            )
    for copy in own_weights:
        copy.start()
    own_table = pltpu.make_async_copy(rbrow, tbls.at[0], sem_tloc.at[0])
    own_table.start()

    barrier = pltpu.get_barrier_semaphore()
    for dz in TABLE_STEPS[1:-1]:
        signal(barrier, (plane(dz) + xc, y))
    for dy in range(1, NY):
        signal(barrier, (me, ypeer(dy)))
    signal_writers(barrier)

    def scale(i, carry):
        row = lax.rsqrt(degree[pl.ds(i, 1), :].astype(F32))
        scal[i] = jnp.transpose(jnp.broadcast_to(row, (TILE, TILE)))
        factor = scal[i]
        for h in range(2):
            feats[0][h][i] = raw[i, :, h * HALF : (h + 1) * HALF] * factor
        return carry

    lax.fori_loop(0, BLK, scale, 0)
    pl.semaphore_wait(barrier, len(TABLE_STEPS) - 2 + NY - 1 + writers)

    table_copies = {
        dz: rdma(rbrow, tblv.at[dz], sem_tsend.at[dz], sem_trecv.at[dz], (plane(dz) + xc, y)) for dz in TABLE_STEPS
    }

    def wait_table(dz):
        table_copies[dz].wait_recv()
        copy = pltpu.make_async_copy(tblv.at[dz], tbls.at[dz], sem_tloc.at[dz])
        copy.start()
        copy.wait()

    def weight_copy(l, h, dy):
        return rdma(
            weights[l].at[pl.ds(h * HALF, HALF)],
            wg[l][h].at[pl.ds(pl.multiple_of(y * HALF, HALF), HALF)],
            sem_wsend.at[l, h, dy - 1],
            sem_wrecv.at[l, h, dy - 1],
            (me, ypeer(dy)),
        )

    def columns(n):
        return pl.ds(pl.multiple_of(n * FEAT, FEAT), FEAT)

    def run_layer(l):
        feat = feats[l]

        def zcopy(h, way, d, part=None):
            src = feat[h] if d == 1 else zbuf[h][way][d - 2]
            dst = zbuf[h][way][d - 1]
            if part is not None:
                blocks = pl.ds(ypeer(part) * MINE, MINE)
                src, dst = src.at[blocks], dst.at[blocks]
            return rdma(
                src,
                dst,
                sem_zsend.at[h, way, d - 1],
                sem_zrecv.at[h, way, d - 1],
                (plane(1 if way == 0 else -1) + xc, y),
            )

        def start_own(h, part=None):
            for way in range(2):
                zcopy(h, way, 1, part).start()

        position = [0, 0]

        def serve(h, dz, ref, far=0):
            slot = plane(dz) + xc
            entry = (-dz) % NZ
            targets = []
            if far:
                targets = [plane(2 * far) + lax.rem(x + dx, NX) * NC + (0 if far > 0 else 1) for dx in range(NX)]
                targets += [plane(far) + seat(dx, dc) for dx, dc in READERS + [(0, 0)]]
            targets += [plane(0) + seat(dx, dc) for dx, dc in READERS]
            base = h * SENDS + position[h]
            position[h] += len(targets)
            for r, target in enumerate(targets):
                sendbuf[base + r] = ref[jnp.minimum(tbls[entry, 0, target], BLK - 1)]
            for r, target in enumerate(targets):
                rdma(
                    sendbuf.at[base + r],
                    inc[h].at[slot],
                    sem_xsend.at[h],
                    sem_xrecv.at[h],
                    (target, y),
                ).start()
            inc[h][slot] = ref[jnp.minimum(tbls[entry, 0, me], BLK - 1)]

        def distance(h, d):
            for way in range(2):
                zcopy(h, way, d).wait_recv()
                if d < NEAR:
                    zcopy(h, way, d + 1).start()
            for way in range(2):
                dz = -d if way == 0 else d
                if l == 0 and h == 0:
                    wait_table(-dz % NZ)
                serve(h, dz, zbuf[h][way][d - 1], (1 if way == 0 else -1) if d == NEAR else 0)

        def ycopy(h, dy):
            n = ypeer(dy)
            return rdma(
                agg[h].at[pl.ds(pl.multiple_of(n * ROWS, ROWS), ROWS)],
                vert[l][h].at[:, pl.ds(pl.multiple_of(y * HALF, HALF), HALF)],
                sem_ysend.at[h, dy - 1],
                sem_yrecv.at[h, dy - 1],
                (me, n),
            )

        def own_tiles(h):
            def step(i, carry):
                agg[h][pl.ds(pl.multiple_of(i * TILE, TILE), TILE), :] = dot3(
                    diag[i], feat[h][i]
                )
                return carry

            lax.fori_loop(0, BLK, step, 0, unroll=2)

        def aggregate(h):
            many = inc[h].at[pl.ds(0, ARRIVALS)]
            pltpu.make_async_copy(many, many, sem_xrecv.at[h]).wait()

            def group(g, carry):
                block_hi, block_lo = split(inc[h][tab[3, g]])
                pair = dot3s(adjhi[g], adjlo[g], block_hi, block_lo)
                prod[2 * g] = pair[:TILE]
                prod[2 * g + 1] = pair[TILE:]
                return carry

            lax.fori_loop(0, GROUPS, group, 0, unroll=4)

            def run(p, acc):
                acc = acc * tab[1, p].astype(F32) + prod[tab[0, p]]
                runs[p] = acc
                return acc

            lax.fori_loop(0, REMOTE, run, jnp.zeros((TILE, HALF), F32), unroll=4)
            for dy in (1, 2, 3, 0):
                n = ypeer(dy)
                for j in range(MINE):
                    i = n * MINE + j
                    rows = pl.ds(pl.multiple_of(i * TILE, TILE), TILE)
                    value = (agg[h][rows, :] + runs[tab[2, i]]) * scal[i]
                    if dy:
                        agg[h][rows, :] = value
                    else:
                        vert[l][h][j * TILE : (j + 1) * TILE, pl.ds(pl.multiple_of(y * HALF, HALF), HALF)] = value
                if dy:
                    ycopy(h, dy).start()

        def wait_inputs(h):
            own_weights[l * 2 + h].wait()
            for dy in range(1, NY):
                weight_copy(l, h, dy).wait_recv()
            for dy in range(1, NY):
                ycopy(h, dy).wait_recv()

        def first_product():
            wait_inputs(0)

            def step(n, carry):
                total[n] = dot3(vert[l][0][...], wg[l][0][:, columns(n)]) + biases[l][:, columns(n)]
                return carry

            lax.fori_loop(0, NY, step, 0)

        def value(n):
            return total[n] + dot3(vert[l][1][...], wg[l][1][:, columns(n)])

        def last_product():
            wait_inputs(1)

            def step(n, carry):
                out[:, columns(n)] = value(n)
                return carry

            lax.fori_loop(0, NY, step, 0)

        def hidden_product():
            wait_inputs(1)
            factor = scal[pl.ds(y * MINE, MINE)]

            def hidden(n):
                found = jnp.maximum(value(n), 0.0).reshape(MINE, TILE, FEAT)
                return found * jnp.concatenate([factor, factor], axis=2)

            def step(k, carry):
                n = ypeer(k + 1)
                hid[n] = hidden(n)
                back(0, k).start()
                return carry

            lax.fori_loop(0, NY - 1, step, 0)
            for k in range(NY - 1):
                back(1, k).start()
            mine = hidden(y)
            for h in range(2):
                feats[1][h][pl.ds(y * MINE, MINE)] = mine[:, :, h * HALF : (h + 1) * HALF]

        def finish_sends():
            for h in range(2):
                for way in range(2):
                    for d in range(1, NEAR + 1):
                        zcopy(h, way, d).wait_send()
                many = sendbuf.at[pl.ds(h * SENDS, SENDS)]
                pltpu.make_async_copy(many, many, sem_xsend.at[h]).wait()

        def finish_exchange():
            for h in range(2):
                for dy in range(1, NY):
                    ycopy(h, dy).wait_send()
                    weight_copy(l, h, dy).wait_send()

        if l == 0:
            for h in range(2):
                start_own(h)
            for copy in table_copies.values():
                copy.start()
            for ll in range(2):
                for h in range(2):
                    for dy in range(1, NY):
                        weight_copy(ll, h, dy).start()
            own_table.wait()
            for h in range(2):
                serve(h, 0, feat[h])
        else:
            pl.semaphore_wait(free, writers)
            for h in range(2):
                start_own(h, 0)
            for h in range(2):
                for k in range(NY - 1):
                    back(h, k).wait()
                    start_own(h, NY - 1 - k)
                serve(h, 0, feat[h])
        if l == 0:
            adj_copy.wait()

            def presplit(g, carry):
                for t in range(2):
                    hi, lo = split(prod[2 * g + t])
                    adjhi[g, t * TILE : (t + 1) * TILE, :] = hi
                    adjlo[g, t * TILE : (t + 1) * TILE, :] = lo
                return carry

            lax.fori_loop(0, GROUPS, presplit, 0)
            runs[REMOTE] = jnp.zeros((TILE, HALF), F32)
        own_tiles(0)
        distance(0, 1)
        distance(1, 1)
        own_tiles(1)
        distance(0, 2)
        distance(1, 2)
        aggregate(0)
        first_product()
        aggregate(1)
        finish_sends()
        if l == 0:
            signal_writers(free)
            hidden_product()
        else:
            last_product()
        finish_exchange()

    def back(h, k):
        n = ypeer(k + 1)
        cols = pl.ds(h * HALF, HALF)
        return rdma(
            hid.at[n, :, :, cols],
            feats[1][h].at[pl.ds(y * MINE, MINE)],
            sem_bsend.at[h, k],
            sem_brecv.at[h, k],
            (me, n),
        )

    run_layer(0)
    run_layer(1)
    for copy in table_copies.values():
        copy.wait_send()


def network(tab, rbrow, degree, features, adj, diag, w1, b1, w2, b2):
    vmem = pl.BlockSpec(memory_space=pltpu.VMEM)
    smem = pl.BlockSpec(memory_space=pltpu.SMEM)
    anyw = pl.BlockSpec(memory_space=pl.ANY)
    dma = pltpu.SemaphoreType.DMA
    return pl.pallas_call(
        both_layers,
        name="both_layers",
        out_shape=jax.ShapeDtypeStruct((ROWS, NY * FEAT), F32),
        in_specs=[smem, vmem, vmem, vmem, anyw, vmem, anyw, vmem, anyw, vmem],
        out_specs=vmem,
        scratch_shapes=[pltpu.VMEM((BLK, TILE, HALF), F32)] * (2 * 2 * NEAR)
        + [pltpu.VMEM((NPARTS, TILE, HALF), F32)] * 2
        + [
            pltpu.VMEM((2 * SENDS, TILE, HALF), F32),
            pltpu.VMEM((REMOTE, TILE, HALF), F32),
            pltpu.VMEM((REMOTE + 1, TILE, HALF), F32),
            pltpu.VMEM((GROUPS, 2 * TILE, TILE), BF16),
            pltpu.VMEM((GROUPS, 2 * TILE, TILE), BF16),
        ]
        + [pltpu.VMEM((NY * ROWS, HALF), F32)] * 2
        + [pltpu.VMEM((ROWS, NY * HALF), F32)] * 4
        + [pltpu.VMEM((NY * HALF, NY * FEAT), F32)] * 4
        + [
            pltpu.VMEM((NY, ROWS, FEAT), F32),
            pltpu.VMEM((NY, MINE, TILE, FEAT), F32),
        ]
        + [pltpu.VMEM((BLK, TILE, HALF), F32)] * 4
        + [
            pltpu.VMEM((BLK, TILE, TILE), F32),
            pltpu.VMEM((NZ, 8, 128), jnp.int32),
            pltpu.SMEM((NZ, 8, 128), jnp.int32),
            dma((NZ,)),
            dma((NZ,)),
            dma((NZ,)),
            dma((2, 2, NEAR)),
            dma((2, 2, NEAR)),
            dma((2,)),
            dma((2,)),
            dma((2, 2, 3)),
            dma((2, 2, 3)),
            dma((2, 2)),
            dma((2, 3)),
            dma((2, 3)),
            dma((2, 3)),
            dma((2, 3)),
            dma,
            pltpu.SemaphoreType.REGULAR,
        ],
        compiler_params=pltpu.CompilerParams(
            collective_id=0, has_side_effects=True, vmem_limit_bytes=67_000_000
        ),
    )(tab, rbrow, degree, features, adj, diag, w1, b1, w2, b2)


def prepare_kernel(tile_src, tile_row, read_block, tab, rbrow, place):
    def clear(i, carry):
        place[i] = 0
        tab[2, i] = REMOTE
        return carry

    lax.fori_loop(0, BLK + 1, clear, 0)

    def count(k, carry):
        r = tile_row[0, k] + 1
        place[r] = place[r] + 1
        return carry

    lax.fori_loop(0, REMOTE, count, 0)

    def accumulate(i, carry):
        place[i] = place[i] + place[i - 1]
        return carry

    lax.fori_loop(1, BLK + 1, accumulate, 0)

    def put(k, carry):
        r = tile_row[0, k]
        p = place[r]
        tab[0, p] = k
        tab[1, p] = (tab[2, r] != REMOTE).astype(jnp.int32)
        tab[2, r] = p
        place[r] = p + 1
        return carry

    lax.fori_loop(0, REMOTE, put, 0)

    def source(g, carry):
        tab[3, g] = tile_src[0, 2 * g]
        return carry

    lax.fori_loop(0, GROUPS, source, 0)
    rbrow[0:1, 0:NPARTS] = read_block[...]


def prepare(tile_src, tile_row, read_block):
    vmem = pl.BlockSpec(memory_space=pltpu.VMEM)
    smem = pl.BlockSpec(memory_space=pltpu.SMEM)
    return pl.pallas_call(
        prepare_kernel,
        name="prepare",
        out_shape=(jax.ShapeDtypeStruct((4, 128), jnp.int32), jax.ShapeDtypeStruct((8, 128), jnp.int32)),
        in_specs=[smem, smem, vmem],
        out_specs=(smem, vmem),
        scratch_shapes=[pltpu.SMEM((BLK + 4,), jnp.int32)],
    )(tile_src, tile_row, read_block)


def per_device(
    features, degree, diag_adj, remote_adj, read_block, tile_src, tile_row, w_first, b_first, w_second, b_second
):
    tab, rbrow = prepare(tile_src, tile_row, read_block)
    return network(
        tab,
        rbrow,
        degree.reshape(BLK, TILE),
        features.reshape(BLK, TILE, FEAT),
        remote_adj[0],
        diag_adj.reshape(BLK, TILE, TILE),
        w_first,
        b_first[None, :],
        w_second,
        b_second[None, :],
    )


def solution(mesh):
    return jax.shard_map(
        per_device,
        mesh=mesh,
        in_specs=(
            P("dom", "feat"),
            P("dom"),
            P("dom", None),
            P("dom", None, None, None),
            P("dom", None),
            P("dom", None),
            P("dom", None),
            P("feat", None),
            P(),
            P("feat", None),
            P(),
        ),
        out_specs=P(("dom", "feat"), None),
        check_vma=False,
    )
```

```python
import functools

import jax
import jax.numpy as jnp
from jax import lax
from jax.experimental import pallas as pl
from jax.experimental.pallas import tpu as pltpu
from jax.sharding import PartitionSpec as P

MESH = pl.DeviceIdType.MESH
F32 = jnp.float32
BF16 = jnp.bfloat16

TILE = 128
BLK = 12
REMOTE = 48
GROUPS = 24
NZ, NX, NC, NY = 8, 4, 2, 4
PLANE = NX * NC
NPARTS = NZ * PLANE
HALF = 128
FEAT = 2 * HALF
NEAR = NZ // 2 - 2
MINE = BLK // NY
ROWS = MINE * TILE
READERS = [(1, 0), (3, 0), (1, 1), (3, 1), (2, 0), (2, 1), (0, 1)]
NREAD = len(READERS)
TABLE_STEPS = [1, 2, NZ - 2, NZ - 1]
SENDS = (1 + 2 * NEAR) * NREAD + 2 * (PLANE + NX)
ARRIVALS = (1 + 2 * NEAR) * NREAD + 2 * PLANE + PLANE


def split(a):
    hi = a.astype(BF16)
    return hi, (a - hi.astype(F32)).astype(BF16)


def dot3s(ah, al, bh, bl):
    out = jnp.dot(ah, bh, preferred_element_type=F32)
    out = out + jnp.dot(ah, bl, preferred_element_type=F32)
    return out + jnp.dot(al, bh, preferred_element_type=F32)


def dot3(a, b):
    return dot3s(*split(a), *split(b))


def both_layers(*refs):
    refs = list(refs)

    def take(n):
        got = refs[:n]
        del refs[:n]
        return got

    tile_src, tile_row, read_block, degree, raw, adj_hbm, diag, w1, b1, w2, b2, out_hbm = take(12)
    zflat = take(2 * 2 * NEAR)
    zbuf = [[[zflat[(h * 2 + way) * NEAR + d] for d in range(NEAR)] for way in range(2)] for h in range(2)]
    inc = take(2)
    sendbuf, prod, runs, adjhi, adjlo = take(5)
    agg = take(2)
    vertflat = take(4)
    vert = [vertflat[:2], vertflat[2:]]
    wgflat = take(4)
    wg = [wgflat[:2], wgflat[2:]]
    total, hid = take(2)
    featflat = take(4)
    feats = [featflat[:2], featflat[2:]]
    scal, tblv, tbls, rbrow, tabv, tab, out, verthi, vertlo = take(9)
    weights = [w1, w2]
    biases = [b1, b2]
    sem_tsend, sem_trecv, sem_tloc, sem_zsend, sem_zrecv, sem_xsend, sem_xrecv = take(7)
    sem_wsend, sem_wrecv, sem_wloc, sem_ysend, sem_yrecv, sem_bsend, sem_brecv, sem_adj, sem_tab, sem_out, free = take(11)

    me = lax.axis_index("dom")
    y = lax.axis_index("feat")
    z = me // PLANE
    xc = lax.rem(me, PLANE)
    x = xc // NC
    c = lax.rem(xc, NC)

    def plane(step):
        return lax.rem(z + (step + NZ), NZ) * PLANE

    def seat(dx, dc):
        return lax.rem(x + dx, NX) * NC + lax.rem(c + dc, NC)

    def ypeer(step):
        return lax.rem(y + step, NY)

    def rdma(src, dst, send, recv, device):
        return pltpu.make_async_remote_copy(
            src_ref=src, dst_ref=dst, send_sem=send, recv_sem=recv, device_id=device, device_id_type=MESH
        )

    def signal(sem, device):
        pl.semaphore_signal(sem, inc=1, device_id=device, device_id_type=MESH)

    def signal_writers(sem):
        for dx, dc in READERS:
            signal(sem, (plane(0) + seat(dx, dc), y))
        beyond = lax.rem(z + (4 * c - 2 + NZ), NZ) * PLANE
        for j in range(PLANE):
            signal(sem, (plane(1) + j, y))
            signal(sem, (plane(-1) + j, y))
            signal(sem, (beyond + j, y))

    writers = NREAD + 3 * PLANE

    adj_copy = pltpu.make_async_copy(adj_hbm, prod, sem_adj)
    adj_copy.start()
    own_weights = []
    for l in range(2):
        for h in range(2):
            own_weights.append(
                pltpu.make_async_copy(
                    weights[l].at[pl.ds(h * HALF, HALF)],
                    wg[l][h].at[pl.ds(pl.multiple_of(y * HALF, HALF), HALF)],
                    sem_wloc.at[l, h],
                )
            )
    for copy in own_weights:
        copy.start()

    rbrow[...] = jnp.zeros((8, TILE), jnp.int32)
    rbrow[0:1, 0:NPARTS] = read_block[...]
    barrier = pltpu.get_barrier_semaphore()
    for dz in TABLE_STEPS[1:-1]:
        signal(barrier, (plane(dz) + xc, y))
    for dy in range(1, NY):
        signal(barrier, (me, ypeer(dy)))
    signal_writers(barrier)

    def scale(i, carry):
        row = lax.rsqrt(degree[pl.ds(i, 1), :].astype(F32))
        scal[i] = jnp.transpose(jnp.broadcast_to(row, (TILE, TILE)))
        factor = scal[i]
        for h in range(2):
            feats[0][h][i] = raw[i, :, h * HALF : (h + 1) * HALF] * factor
        return carry

    lax.fori_loop(0, BLK, scale, 0)
    pl.semaphore_wait(barrier, len(TABLE_STEPS) - 2 + NY - 1 + writers)

    table_copies = {
        dz: rdma(rbrow, tblv.at[dz], sem_tsend.at[dz], sem_trecv.at[dz], (plane(dz) + xc, y)) for dz in TABLE_STEPS
    }

    own_table = pltpu.make_async_copy(rbrow, tbls.at[0], sem_tloc.at[0])
    own_table.start()

    def wait_table(dz):
        table_copies[dz].wait_recv()
        copy = pltpu.make_async_copy(tblv.at[dz], tbls.at[dz], sem_tloc.at[dz])
        copy.start()
        copy.wait()

    def sort_tiles():
        lane = lax.broadcasted_iota(jnp.int32, (TILE, TILE), 1)
        sublane = lax.broadcasted_iota(jnp.int32, (TILE, TILE), 0)
        tabv[...] = jnp.full((8, TILE), BLK + 1, jnp.int32)
        tabv[0:1, 0:REMOTE] = tile_row[...]
        rows = jnp.broadcast_to(tabv[0:1, :], (TILE, TILE))
        rows_down = jnp.transpose(rows)
        key, key_down = rows * TILE + lane, rows_down * TILE + sublane

        def total_of(mask, what):
            return jnp.sum(jnp.where(mask, what, 0), axis=0, keepdims=True)

        rank = total_of(key_down < key, jnp.ones_like(key))
        rank_down = jnp.transpose(jnp.broadcast_to(rank, (TILE, TILE)))
        perm = total_of(rank_down == lane, sublane)
        row = total_of(rank_down == lane, rows_down)
        before = total_of(rank_down == lane - 1, rows_down)
        upto = total_of(rows_down <= lane, jnp.ones_like(key))
        here = total_of(rows_down == lane, jnp.ones_like(key))
        tabv[0:1, :] = perm
        tabv[1:2, :] = jnp.where((row == before) & (lane[0:1] > 0), 1, 0)
        tabv[2:3, :] = jnp.where(here > 0, upto - 1, REMOTE)
        copy = pltpu.make_async_copy(tabv, tab, sem_tab)
        copy.start()
        copy.wait()

    def weight_copy(l, h, dy):
        return rdma(
            weights[l].at[pl.ds(h * HALF, HALF)],
            wg[l][h].at[pl.ds(pl.multiple_of(y * HALF, HALF), HALF)],
            sem_wsend.at[l, h, dy - 1],
            sem_wrecv.at[l, h, dy - 1],
            (me, ypeer(dy)),
        )

    def columns(n):
        return pl.ds(pl.multiple_of(n * FEAT, FEAT), FEAT)

    def run_layer(l):
        feat = feats[l]

        def zcopy(h, way, d, part=None):
            src = feat[h] if d == 1 else zbuf[h][way][d - 2]
            dst = zbuf[h][way][d - 1]
            if part is not None:
                blocks = pl.ds(ypeer(part) * MINE, MINE)
                src, dst = src.at[blocks], dst.at[blocks]
            return rdma(
                src,
                dst,
                sem_zsend.at[h, way, d - 1],
                sem_zrecv.at[h, way, d - 1],
                (plane(1 if way == 0 else -1) + xc, y),
            )

        def start_own(h, part=None):
            for way in range(2):
                zcopy(h, way, 1, part).start()

        position = [0, 0]

        def serve(h, dz, ref, far=0):
            slot = plane(dz) + xc
            entry = (-dz) % NZ
            targets = []
            if far:
                targets = [plane(far) + seat(dx, dc) for dx, dc in READERS + [(0, 0)]]
                targets += [plane(2 * far) + lax.rem(x + dx, NX) * NC + (0 if far > 0 else 1) for dx in range(NX)]
            targets += [plane(0) + seat(dx, dc) for dx, dc in READERS]
            base = h * SENDS + position[h]
            position[h] += len(targets)
            for r, target in enumerate(targets):
                sendbuf[base + r] = ref[jnp.minimum(tbls[entry, 0, target], BLK - 1)]
            for r, target in enumerate(targets):
                rdma(
                    sendbuf.at[base + r],
                    inc[h].at[slot],
                    sem_xsend.at[h],
                    sem_xrecv.at[h],
                    (target, y),
                ).start()
            inc[h][slot] = ref[jnp.minimum(tbls[entry, 0, me], BLK - 1)]

        def distance(h, d):
            for way in range(2):
                zcopy(h, way, d).wait_recv()
                if d < NEAR:
                    zcopy(h, way, d + 1).start()
            for way in range(2):
                dz = -d if way == 0 else d
                if l == 0 and h == 0:
                    wait_table(-dz % NZ)
                serve(h, dz, zbuf[h][way][d - 1], (1 if way == 0 else -1) if d == NEAR else 0)

        def ycopy(h, dy):
            n = ypeer(dy)
            return rdma(
                agg[h].at[pl.ds(pl.multiple_of(n * ROWS, ROWS), ROWS)],
                vert[l][h].at[:, pl.ds(pl.multiple_of(y * HALF, HALF), HALF)],
                sem_ysend.at[h, dy - 1],
                sem_yrecv.at[h, dy - 1],
                (me, n),
            )

        def own_tiles(h):
            def step(i, carry):
                agg[h][pl.ds(pl.multiple_of(i * TILE, TILE), TILE), :] = dot3(
                    diag[i], feat[h][i]
                )
                return carry

            lax.fori_loop(0, BLK, step, 0, unroll=2)

        def aggregate(h):
            many = inc[h].at[pl.ds(0, ARRIVALS)]
            pltpu.make_async_copy(many, many, sem_xrecv.at[h]).wait()

            def group(g, carry):
                block_hi, block_lo = split(inc[h][tile_src[0, 2 * g]])
                pair = dot3s(adjhi[g], adjlo[g], block_hi, block_lo)
                prod[2 * g] = pair[:TILE]
                prod[2 * g + 1] = pair[TILE:]
                return carry

            lax.fori_loop(0, GROUPS, group, 0, unroll=4)

            def run(p, acc):
                acc = acc * tab[1, p].astype(F32) + prod[tab[0, p]]
                runs[p] = acc
                return acc

            lax.fori_loop(0, REMOTE, run, jnp.zeros((TILE, HALF), F32), unroll=4)
            for dy in (1, 2, 3, 0):
                n = ypeer(dy)
                for j in range(MINE):
                    i = n * MINE + j
                    rows = pl.ds(pl.multiple_of(i * TILE, TILE), TILE)
                    value = (agg[h][rows, :] + runs[tab[2, i]]) * scal[i]
                    if dy:
                        agg[h][rows, :] = value
                    else:
                        vert[l][h][j * TILE : (j + 1) * TILE, pl.ds(pl.multiple_of(y * HALF, HALF), HALF)] = value
                if dy:
                    ycopy(h, dy).start()

        def wait_inputs(h):
            own_weights[l * 2 + h].wait()
            for dy in range(1, NY):
                weight_copy(l, h, dy).wait_recv()
            for dy in range(1, NY):
                ycopy(h, dy).wait_recv()

        def load_inputs(h):
            wait_inputs(h)
            hi, lo = split(vert[l][h][...])
            verthi[...] = hi
            vertlo[...] = lo

        def product(h, n):
            return dot3s(verthi[...], vertlo[...], *split(wg[l][h][:, columns(n)]))

        def first_product():
            load_inputs(0)

            def step(n, carry):
                total[n] = product(0, n) + biases[l][:, columns(n)]
                return carry

            lax.fori_loop(0, NY, step, 0)

        def value(n):
            return total[n] + product(1, n)

        def write(n):
            return pltpu.make_async_copy(out.at[:, columns(n)], out_hbm.at[:, columns(n)], sem_out.at[n])

        def last_product():
            load_inputs(1)

            def step(n, carry):
                out[:, columns(n)] = value(n)
                write(n).start()
                return carry

            lax.fori_loop(0, NY, step, 0)
            for n in range(NY):
                write(n).wait()

        def hidden_product():
            load_inputs(1)
            factor = scal[pl.ds(y * MINE, MINE)]

            def hidden(n):
                found = jnp.maximum(value(n), 0.0).reshape(MINE, TILE, FEAT)
                return found * jnp.concatenate([factor, factor], axis=2)

            def step(k, carry):
                n = ypeer(k + 1)
                hid[n] = hidden(n)
                back(0, k).start()
                return carry

            lax.fori_loop(0, NY - 1, step, 0)
            for k in range(NY - 1):
                back(1, k).start()
            mine = hidden(y)
            for h in range(2):
                feats[1][h][pl.ds(y * MINE, MINE)] = mine[:, :, h * HALF : (h + 1) * HALF]

        def finish_sends():
            for h in range(2):
                for way in range(2):
                    for d in range(1, NEAR + 1):
                        zcopy(h, way, d).wait_send()
                many = sendbuf.at[pl.ds(h * SENDS, SENDS)]
                pltpu.make_async_copy(many, many, sem_xsend.at[h]).wait()

        def finish_exchange():
            for h in range(2):
                for dy in range(1, NY):
                    ycopy(h, dy).wait_send()
                    weight_copy(l, h, dy).wait_send()

        if l == 0:
            for h in range(2):
                start_own(h)
            for copy in table_copies.values():
                copy.start()
            for ll in range(2):
                for h in range(2):
                    for dy in range(1, NY):
                        weight_copy(ll, h, dy).start()
            own_table.wait()
            for h in range(2):
                serve(h, 0, feat[h])
        else:
            pl.semaphore_wait(free, writers)
            for h in range(2):
                start_own(h, 0)
            for h in range(2):
                for k in range(NY - 1):
                    back(h, k).wait()
                    start_own(h, NY - 1 - k)
                serve(h, 0, feat[h])
        if l == 0:
            adj_copy.wait()

            def presplit(g, carry):
                for t in range(2):
                    hi, lo = split(prod[2 * g + t])
                    adjhi[g, t * TILE : (t + 1) * TILE, :] = hi
                    adjlo[g, t * TILE : (t + 1) * TILE, :] = lo
                return carry

            lax.fori_loop(0, GROUPS, presplit, 0)
            runs[REMOTE] = jnp.zeros((TILE, HALF), F32)
        own_tiles(0)
        if l == 0:
            sort_tiles()
        distance(0, 1)
        distance(1, 1)
        own_tiles(1)
        distance(0, 2)
        distance(1, 2)
        aggregate(0)
        first_product()
        aggregate(1)
        finish_sends()
        if l == 0:
            signal_writers(free)
            hidden_product()
        else:
            last_product()
        finish_exchange()

    def back(h, k):
        n = ypeer(k + 1)
        cols = pl.ds(h * HALF, HALF)
        return rdma(
            hid.at[n, :, :, cols],
            feats[1][h].at[pl.ds(y * MINE, MINE)],
            sem_bsend.at[h, k],
            sem_brecv.at[h, k],
            (me, n),
        )

    run_layer(0)
    run_layer(1)
    for copy in table_copies.values():
        copy.wait_send()


def network(*operands):
    vmem = pl.BlockSpec(memory_space=pltpu.VMEM)
    smem = pl.BlockSpec(memory_space=pltpu.SMEM)
    anyw = pl.BlockSpec(memory_space=pl.ANY)
    dma = pltpu.SemaphoreType.DMA
    return pl.pallas_call(
        both_layers,
        name="both_layers",
        out_shape=jax.ShapeDtypeStruct((ROWS, NY * FEAT), F32),
        in_specs=[smem, vmem, vmem, vmem, vmem, anyw, vmem, anyw, vmem, anyw, vmem],
        out_specs=anyw,
        scratch_shapes=[pltpu.VMEM((BLK, TILE, HALF), F32)] * (2 * 2 * NEAR)
        + [pltpu.VMEM((NPARTS, TILE, HALF), F32)] * 2
        + [
            pltpu.VMEM((2 * SENDS, TILE, HALF), F32),
            pltpu.VMEM((REMOTE, TILE, HALF), F32),
            pltpu.VMEM((REMOTE + 1, TILE, HALF), F32),
            pltpu.VMEM((GROUPS, 2 * TILE, TILE), BF16),
            pltpu.VMEM((GROUPS, 2 * TILE, TILE), BF16),
        ]
        + [pltpu.VMEM((NY * ROWS, HALF), F32)] * 2
        + [pltpu.VMEM((ROWS, NY * HALF), F32)] * 4
        + [pltpu.VMEM((NY * HALF, NY * FEAT), F32)] * 4
        + [
            pltpu.VMEM((NY, ROWS, FEAT), F32),
            pltpu.VMEM((NY, MINE, TILE, FEAT), F32),
        ]
        + [pltpu.VMEM((BLK, TILE, HALF), F32)] * 4
        + [
            pltpu.VMEM((BLK, TILE, TILE), F32),
            pltpu.VMEM((NZ, 8, 128), jnp.int32),
            pltpu.SMEM((NZ, 8, 128), jnp.int32),
            pltpu.VMEM((8, TILE), jnp.int32),
            pltpu.VMEM((8, TILE), jnp.int32),
            pltpu.SMEM((8, TILE), jnp.int32),
            pltpu.VMEM((ROWS, NY * FEAT), F32),
            pltpu.VMEM((ROWS, NY * HALF), BF16),
            pltpu.VMEM((ROWS, NY * HALF), BF16),
            dma((NZ,)),
            dma((NZ,)),
            dma((NZ,)),
            dma((2, 2, NEAR)),
            dma((2, 2, NEAR)),
            dma((2,)),
            dma((2,)),
            dma((2, 2, 3)),
            dma((2, 2, 3)),
            dma((2, 2)),
            dma((2, 3)),
            dma((2, 3)),
            dma((2, 3)),
            dma((2, 3)),
            dma,
            dma,
            dma((NY,)),
            pltpu.SemaphoreType.REGULAR,
        ],
        compiler_params=pltpu.CompilerParams(
            collective_id=0, has_side_effects=True, vmem_limit_bytes=67_000_000
        ),
    )(*operands)


def per_device(
    features, degree, diag_adj, remote_adj, read_block, tile_src, tile_row, w_first, b_first, w_second, b_second
):
    return network(
        tile_src,
        tile_row,
        read_block,
        degree.reshape(BLK, TILE),
        features.reshape(BLK, TILE, FEAT),
        remote_adj[0],
        diag_adj.reshape(BLK, TILE, TILE),
        w_first,
        b_first[None, :],
        w_second,
        b_second[None, :],
    )


def solution(mesh):
    return jax.shard_map(
        per_device,
        mesh=mesh,
        in_specs=(
            P("dom", "feat"),
            P("dom"),
            P("dom", None),
            P("dom", None, None, None),
            P("dom", None),
            P("dom", None),
            P("dom", None),
            P("feat", None),
            P(),
            P("feat", None),
            P(),
        ),
        out_specs=P(("dom", "feat"), None),
        check_vma=False,
    )
```

```python
import functools

import jax
import jax.numpy as jnp
from jax import lax
from jax.experimental import pallas as pl
from jax.experimental.pallas import tpu as pltpu
from jax.sharding import PartitionSpec as P

MESH = pl.DeviceIdType.MESH
F32 = jnp.float32
BF16 = jnp.bfloat16

TILE = 128
BLK = 12
REMOTE = 48
GROUPS = 24
NZ, NX, NC, NY = 8, 4, 2, 4
PLANE = NX * NC
NPARTS = NZ * PLANE
HALF = 128
FEAT = 2 * HALF
NEAR = NZ // 2 - 2
MINE = BLK // NY
ROWS = MINE * TILE
READERS = [(1, 0), (3, 0), (1, 1), (3, 1), (2, 0), (2, 1), (0, 1)]
NREAD = len(READERS)
TABLE_STEPS = [1, 2, NZ - 2, NZ - 1]
SENDS = (1 + 2 * NEAR) * NREAD + 2 * (PLANE + NX)
ARRIVALS = (1 + 2 * NEAR) * NREAD + 2 * PLANE + PLANE


def split(a):
    hi = a.astype(BF16)
    return hi, (a - hi.astype(F32)).astype(BF16)


def dot3s(ah, al, bh, bl):
    out = jnp.dot(ah, bh, preferred_element_type=F32)
    out = out + jnp.dot(ah, bl, preferred_element_type=F32)
    return out + jnp.dot(al, bh, preferred_element_type=F32)


def dot3(a, b):
    return dot3s(*split(a), *split(b))


def both_layers(*refs):
    refs = list(refs)

    def take(n):
        got = refs[:n]
        del refs[:n]
        return got

    tile_src, tile_row, read_block, degree, raw, adj_hbm, diag, w1, b1, w2, b2, out_hbm = take(12)
    zflat = take(2 * 2 * NEAR)
    zbuf = [[[zflat[(h * 2 + way) * NEAR + d] for d in range(NEAR)] for way in range(2)] for h in range(2)]
    inc = take(2)
    sendbuf, prod, runs, adjhi, adjlo = take(5)
    agg = take(2)
    vertflat = take(4)
    vert = [vertflat[:2], vertflat[2:]]
    wgflat = take(4)
    wg = [wgflat[:2], wgflat[2:]]
    total, hid = take(2)
    featflat = take(4)
    feats = [featflat[:2], featflat[2:]]
    scal, tblv, tbls, rbrow, tabv, tab, out, verthi, vertlo = take(9)
    weights = [w1, w2]
    biases = [b1, b2]
    sem_tsend, sem_trecv, sem_tloc, sem_zsend, sem_zrecv, sem_xsend, sem_xrecv = take(7)
    sem_wsend, sem_wrecv, sem_wloc, sem_ysend, sem_yrecv, sem_bsend, sem_brecv, sem_adj, sem_tab, sem_out, free = take(11)

    me = lax.axis_index("dom")
    y = lax.axis_index("feat")
    z = me // PLANE
    xc = lax.rem(me, PLANE)
    x = xc // NC
    c = lax.rem(xc, NC)

    def plane(step):
        return lax.rem(z + (step + NZ), NZ) * PLANE

    def seat(dx, dc):
        return lax.rem(x + dx, NX) * NC + lax.rem(c + dc, NC)

    def ypeer(step):
        return lax.rem(y + step, NY)

    def rdma(src, dst, send, recv, device):
        return pltpu.make_async_remote_copy(
            src_ref=src, dst_ref=dst, send_sem=send, recv_sem=recv, device_id=device, device_id_type=MESH
        )

    def signal(sem, device):
        pl.semaphore_signal(sem, inc=1, device_id=device, device_id_type=MESH)

    def signal_writers(sem):
        for dx, dc in READERS:
            signal(sem, (plane(0) + seat(dx, dc), y))
        beyond = lax.rem(z + (4 * c - 2 + NZ), NZ) * PLANE
        for j in range(PLANE):
            signal(sem, (plane(1) + j, y))
            signal(sem, (plane(-1) + j, y))
            signal(sem, (beyond + j, y))

    writers = NREAD + 3 * PLANE

    adj_copy = pltpu.make_async_copy(adj_hbm, prod, sem_adj)
    adj_copy.start()
    own_weights = []
    for l in range(2):
        for h in range(2):
            own_weights.append(
                pltpu.make_async_copy(
                    weights[l].at[pl.ds(h * HALF, HALF)],
                    wg[l][h].at[pl.ds(pl.multiple_of(y * HALF, HALF), HALF)],
                    sem_wloc.at[l, h],
                )
            )
    for copy in own_weights:
        copy.start()

    rbrow[...] = jnp.zeros((8, TILE), jnp.int32)
    rbrow[0:1, 0:NPARTS] = read_block[...]
    barrier = pltpu.get_barrier_semaphore()
    for dz in TABLE_STEPS[1:-1]:
        signal(barrier, (plane(dz) + xc, y))
    for dy in range(1, NY):
        signal(barrier, (me, ypeer(dy)))
    signal_writers(barrier)

    def scale(i, carry):
        row = lax.rsqrt(degree[pl.ds(i, 1), :].astype(F32))
        scal[i] = jnp.transpose(jnp.broadcast_to(row, (TILE, TILE)))
        factor = scal[i]
        for h in range(2):
            feats[0][h][i] = raw[i, :, h * HALF : (h + 1) * HALF] * factor
        return carry

    lax.fori_loop(0, BLK, scale, 0)
    pl.semaphore_wait(barrier, len(TABLE_STEPS) - 2 + NY - 1 + writers)

    table_copies = {
        dz: rdma(rbrow, tblv.at[dz], sem_tsend.at[dz], sem_trecv.at[dz], (plane(dz) + xc, y)) for dz in TABLE_STEPS
    }

    own_table = pltpu.make_async_copy(rbrow, tbls.at[0], sem_tloc.at[0])
    own_table.start()

    def wait_table(dz):
        table_copies[dz].wait_recv()
        copy = pltpu.make_async_copy(tblv.at[dz], tbls.at[dz], sem_tloc.at[dz])
        copy.start()
        copy.wait()

    def sort_tiles():
        lane = lax.broadcasted_iota(jnp.int32, (TILE, TILE), 1)
        sublane = lax.broadcasted_iota(jnp.int32, (TILE, TILE), 0)
        tabv[...] = jnp.full((8, TILE), BLK + 1, jnp.int32)
        tabv[0:1, 0:REMOTE] = tile_row[...]
        rows = jnp.broadcast_to(tabv[0:1, :], (TILE, TILE))
        rows_down = jnp.transpose(rows)
        key, key_down = rows * TILE + lane, rows_down * TILE + sublane

        def total_of(mask, what):
            return jnp.sum(jnp.where(mask, what, 0), axis=0, keepdims=True)

        rank = total_of(key_down < key, jnp.ones_like(key))
        rank_down = jnp.transpose(jnp.broadcast_to(rank, (TILE, TILE)))
        perm = total_of(rank_down == lane, sublane)
        row = total_of(rank_down == lane, rows_down)
        before = total_of(rank_down == lane - 1, rows_down)
        upto = total_of(rows_down <= lane, jnp.ones_like(key))
        here = total_of(rows_down == lane, jnp.ones_like(key))
        tabv[0:1, :] = perm
        tabv[1:2, :] = jnp.where((row == before) & (lane[0:1] > 0), 1, 0)
        tabv[2:3, :] = jnp.where(here > 0, upto - 1, REMOTE)
        copy = pltpu.make_async_copy(tabv, tab, sem_tab)
        copy.start()
        copy.wait()

    def weight_copy(l, h, dy):
        return rdma(
            weights[l].at[pl.ds(h * HALF, HALF)],
            wg[l][h].at[pl.ds(pl.multiple_of(y * HALF, HALF), HALF)],
            sem_wsend.at[l, h, dy - 1],
            sem_wrecv.at[l, h, dy - 1],
            (me, ypeer(dy)),
        )

    def columns(n):
        return pl.ds(pl.multiple_of(n * FEAT, FEAT), FEAT)

    def zcopy(l, h, way, d, part=None):
        src = feats[l][h] if d == 1 else zbuf[h][way][d - 2]
        dst = zbuf[h][way][d - 1]
        if part is not None:
            blocks = pl.ds(ypeer(part) * MINE, MINE)
            src, dst = src.at[blocks], dst.at[blocks]
        return rdma(
            src,
            dst,
            sem_zsend.at[h, way, d - 1],
            sem_zrecv.at[h, way, d - 1],
            (plane(1 if way == 0 else -1) + xc, y),
        )

    def start_own(l, h, part=None):
        for way in range(2):
            zcopy(l, h, way, 1, part).start()

    def run_layer(l):
        feat = feats[l]

        position = [0, 0]

        def serve(h, dz, ref, far=0):
            slot = plane(dz) + xc
            entry = (-dz) % NZ
            targets = []
            if far:
                targets = [plane(far) + seat(dx, dc) for dx, dc in READERS + [(0, 0)]]
                targets += [plane(2 * far) + lax.rem(x + dx, NX) * NC + (0 if far > 0 else 1) for dx in range(NX)]
            targets += [plane(0) + seat(dx, dc) for dx, dc in READERS]
            base = h * SENDS + position[h]
            position[h] += len(targets)
            for r, target in enumerate(targets):
                sendbuf[base + r] = ref[jnp.minimum(tbls[entry, 0, target], BLK - 1)]
            for r, target in enumerate(targets):
                rdma(
                    sendbuf.at[base + r],
                    inc[h].at[slot],
                    sem_xsend.at[h],
                    sem_xrecv.at[h],
                    (target, y),
                ).start()
            inc[h][slot] = ref[jnp.minimum(tbls[entry, 0, me], BLK - 1)]

        def distance(h, d):
            for way in range(2):
                zcopy(l, h, way, d).wait_recv()
                if d < NEAR:
                    zcopy(l, h, way, d + 1).start()
            for way in range(2):
                dz = -d if way == 0 else d
                if l == 0 and h == 0:
                    wait_table(-dz % NZ)
                serve(h, dz, zbuf[h][way][d - 1], (1 if way == 0 else -1) if d == NEAR else 0)

        def ycopy(h, dy):
            n = ypeer(dy)
            return rdma(
                agg[h].at[pl.ds(pl.multiple_of(n * ROWS, ROWS), ROWS)],
                vert[l][h].at[:, pl.ds(pl.multiple_of(y * HALF, HALF), HALF)],
                sem_ysend.at[h, dy - 1],
                sem_yrecv.at[h, dy - 1],
                (me, n),
            )

        def own_tiles(h):
            def step(i, carry):
                agg[h][pl.ds(pl.multiple_of(i * TILE, TILE), TILE), :] = dot3(
                    diag[i], feat[h][i]
                )
                return carry

            lax.fori_loop(0, BLK, step, 0, unroll=2)

        def aggregate(h):
            many = inc[h].at[pl.ds(0, ARRIVALS)]
            pltpu.make_async_copy(many, many, sem_xrecv.at[h]).wait()

            def group(g, carry):
                block_hi, block_lo = split(inc[h][tile_src[0, 2 * g]])
                pair = dot3s(adjhi[g], adjlo[g], block_hi, block_lo)
                prod[2 * g] = pair[:TILE]
                prod[2 * g + 1] = pair[TILE:]
                return carry

            lax.fori_loop(0, GROUPS, group, 0, unroll=8)

            def run(p, acc):
                acc = acc * tab[1, p].astype(F32) + prod[tab[0, p]]
                runs[p] = acc
                return acc

            lax.fori_loop(0, REMOTE, run, jnp.zeros((TILE, HALF), F32), unroll=8)
            for dy in (1, 2, 3, 0):
                n = ypeer(dy)
                for j in range(MINE):
                    i = n * MINE + j
                    rows = pl.ds(pl.multiple_of(i * TILE, TILE), TILE)
                    value = (agg[h][rows, :] + runs[tab[2, i]]) * scal[i]
                    if dy:
                        agg[h][rows, :] = value
                    else:
                        vert[l][h][j * TILE : (j + 1) * TILE, pl.ds(pl.multiple_of(y * HALF, HALF), HALF)] = value
                if dy:
                    ycopy(h, dy).start()

        def wait_inputs(h):
            own_weights[l * 2 + h].wait()
            for dy in range(1, NY):
                weight_copy(l, h, dy).wait_recv()
            for dy in range(1, NY):
                ycopy(h, dy).wait_recv()

        def load_inputs(h):
            wait_inputs(h)
            hi, lo = split(vert[l][h][...])
            verthi[...] = hi
            vertlo[...] = lo

        def product(h, n):
            return dot3s(verthi[...], vertlo[...], *split(wg[l][h][:, columns(n)]))

        def first_product():
            load_inputs(0)

            def step(n, carry):
                total[n] = product(0, n) + biases[l][:, columns(n)]
                return carry

            lax.fori_loop(0, NY, step, 0)

        def value(n):
            return total[n] + product(1, n)

        def write(n):
            return pltpu.make_async_copy(out.at[:, columns(n)], out_hbm.at[:, columns(n)], sem_out.at[n])

        def last_product():
            load_inputs(1)

            def step(n, carry):
                out[:, columns(n)] = value(n)
                write(n).start()
                return carry

            lax.fori_loop(0, NY, step, 0)
            for n in range(NY):
                write(n).wait()

        def hidden_product():
            load_inputs(1)
            factor = scal[pl.ds(y * MINE, MINE)]

            def hidden(n):
                found = jnp.maximum(value(n), 0.0).reshape(MINE, TILE, FEAT)
                return found * jnp.concatenate([factor, factor], axis=2)

            def step(k, carry):
                n = ypeer(k + 1)
                hid[n] = hidden(n)
                back(0, k).start()
                return carry

            mine = hidden(y)
            for h in range(2):
                feats[1][h][pl.ds(y * MINE, MINE)] = mine[:, :, h * HALF : (h + 1) * HALF]
            lax.fori_loop(0, 1, step, 0)
            pl.semaphore_wait(free, writers)
            for h in range(2):
                start_own(1, h, 0)
            lax.fori_loop(1, NY - 1, step, 0)
            for k in range(NY - 1):
                back(1, k).start()

        def finish_sends():
            for h in range(2):
                for way in range(2):
                    for d in range(1, NEAR + 1):
                        zcopy(l, h, way, d).wait_send()
                many = sendbuf.at[pl.ds(h * SENDS, SENDS)]
                pltpu.make_async_copy(many, many, sem_xsend.at[h]).wait()

        def finish_exchange():
            for h in range(2):
                for dy in range(1, NY):
                    ycopy(h, dy).wait_send()
                    weight_copy(l, h, dy).wait_send()

        if l == 0:
            for h in range(2):
                start_own(l, h)
            for copy in table_copies.values():
                copy.start()
            for ll in range(2):
                for h in range(2):
                    for dy in range(1, NY):
                        weight_copy(ll, h, dy).start()
            own_table.wait()
            for h in range(2):
                serve(h, 0, feat[h])
        else:
            for h in range(2):
                for k in range(NY - 1):
                    back(h, k).wait()
                    start_own(l, h, NY - 1 - k)
                serve(h, 0, feat[h])
        if l == 0:
            adj_copy.wait()

            def presplit(g, carry):
                for t in range(2):
                    hi, lo = split(prod[2 * g + t])
                    adjhi[g, t * TILE : (t + 1) * TILE, :] = hi
                    adjlo[g, t * TILE : (t + 1) * TILE, :] = lo
                return carry

            lax.fori_loop(0, GROUPS, presplit, 0)
            runs[REMOTE] = jnp.zeros((TILE, HALF), F32)
        own_tiles(0)
        if l == 0:
            sort_tiles()
        distance(0, 1)
        distance(1, 1)
        own_tiles(1)
        distance(0, 2)
        distance(1, 2)
        aggregate(0)
        first_product()
        aggregate(1)
        finish_sends()
        if l == 0:
            signal_writers(free)
            hidden_product()
        else:
            last_product()
        finish_exchange()

    def back(h, k):
        n = ypeer(k + 1)
        cols = pl.ds(h * HALF, HALF)
        return rdma(
            hid.at[n, :, :, cols],
            feats[1][h].at[pl.ds(y * MINE, MINE)],
            sem_bsend.at[h, k],
            sem_brecv.at[h, k],
            (me, n),
        )

    run_layer(0)
    run_layer(1)
    for copy in table_copies.values():
        copy.wait_send()


def network(*operands):
    vmem = pl.BlockSpec(memory_space=pltpu.VMEM)
    smem = pl.BlockSpec(memory_space=pltpu.SMEM)
    anyw = pl.BlockSpec(memory_space=pl.ANY)
    dma = pltpu.SemaphoreType.DMA
    return pl.pallas_call(
        both_layers,
        name="both_layers",
        out_shape=jax.ShapeDtypeStruct((ROWS, NY * FEAT), F32),
        in_specs=[smem, vmem, vmem, vmem, vmem, anyw, vmem, anyw, vmem, anyw, vmem],
        out_specs=anyw,
        scratch_shapes=[pltpu.VMEM((BLK, TILE, HALF), F32)] * (2 * 2 * NEAR)
        + [pltpu.VMEM((NPARTS, TILE, HALF), F32)] * 2
        + [
            pltpu.VMEM((2 * SENDS, TILE, HALF), F32),
            pltpu.VMEM((REMOTE, TILE, HALF), F32),
            pltpu.VMEM((REMOTE + 1, TILE, HALF), F32),
            pltpu.VMEM((GROUPS, 2 * TILE, TILE), BF16),
            pltpu.VMEM((GROUPS, 2 * TILE, TILE), BF16),
        ]
        + [pltpu.VMEM((NY * ROWS, HALF), F32)] * 2
        + [pltpu.VMEM((ROWS, NY * HALF), F32)] * 4
        + [pltpu.VMEM((NY * HALF, NY * FEAT), F32)] * 4
        + [
            pltpu.VMEM((NY, ROWS, FEAT), F32),
            pltpu.VMEM((NY, MINE, TILE, FEAT), F32),
        ]
        + [pltpu.VMEM((BLK, TILE, HALF), F32)] * 4
        + [
            pltpu.VMEM((BLK, TILE, TILE), F32),
            pltpu.VMEM((NZ, 8, 128), jnp.int32),
            pltpu.SMEM((NZ, 8, 128), jnp.int32),
            pltpu.VMEM((8, TILE), jnp.int32),
            pltpu.VMEM((8, TILE), jnp.int32),
            pltpu.SMEM((8, TILE), jnp.int32),
            pltpu.VMEM((ROWS, NY * FEAT), F32),
            pltpu.VMEM((ROWS, NY * HALF), BF16),
            pltpu.VMEM((ROWS, NY * HALF), BF16),
            dma((NZ,)),
            dma((NZ,)),
            dma((NZ,)),
            dma((2, 2, NEAR)),
            dma((2, 2, NEAR)),
            dma((2,)),
            dma((2,)),
            dma((2, 2, 3)),
            dma((2, 2, 3)),
            dma((2, 2)),
            dma((2, 3)),
            dma((2, 3)),
            dma((2, 3)),
            dma((2, 3)),
            dma,
            dma,
            dma((NY,)),
            pltpu.SemaphoreType.REGULAR,
        ],
        compiler_params=pltpu.CompilerParams(
            collective_id=0, has_side_effects=True, vmem_limit_bytes=67_000_000
        ),
    )(*operands)


def per_device(
    features, degree, diag_adj, remote_adj, read_block, tile_src, tile_row, w_first, b_first, w_second, b_second
):
    return network(
        tile_src,
        tile_row,
        read_block,
        degree.reshape(BLK, TILE),
        features.reshape(BLK, TILE, FEAT),
        remote_adj[0],
        diag_adj.reshape(BLK, TILE, TILE),
        w_first,
        b_first[None, :],
        w_second,
        b_second[None, :],
    )


def solution(mesh):
    return jax.shard_map(
        per_device,
        mesh=mesh,
        in_specs=(
            P("dom", "feat"),
            P("dom"),
            P("dom", None),
            P("dom", None, None, None),
            P("dom", None),
            P("dom", None),
            P("dom", None),
            P("feat", None),
            P(),
            P("feat", None),
            P(),
        ),
        out_specs=P(("dom", "feat"), None),
        check_vma=False,
    )
```

```python
import functools

import jax
import jax.numpy as jnp
from jax import lax
from jax.experimental import pallas as pl
from jax.experimental.pallas import tpu as pltpu
from jax.sharding import PartitionSpec as P

MESH = pl.DeviceIdType.MESH
F32 = jnp.float32
BF16 = jnp.bfloat16

TILE = 128
BLK = 12
REMOTE = 48
GROUPS = 24
NZ, NX, NC, NY = 8, 4, 2, 4
PLANE = NX * NC
NPARTS = NZ * PLANE
HALF = 128
FEAT = 2 * HALF
NEAR = NZ // 2 - 2
MINE = BLK // NY
ROWS = MINE * TILE
READERS = [(1, 0), (3, 0), (1, 1), (3, 1), (2, 0), (2, 1), (0, 1)]
NREAD = len(READERS)
TABLE_STEPS = [1, 2, NZ - 2, NZ - 1]
SENDS = (1 + 2 * NEAR) * NREAD + 2 * (PLANE + NX)
ARRIVALS = (1 + 2 * NEAR) * NREAD + 2 * PLANE + PLANE


def split(a):
    hi = a.astype(BF16)
    return hi, (a - hi.astype(F32)).astype(BF16)


def dot3s(ah, al, bh, bl):
    out = jnp.dot(ah, bh, preferred_element_type=F32)
    out = out + jnp.dot(ah, bl, preferred_element_type=F32)
    return out + jnp.dot(al, bh, preferred_element_type=F32)


def dot3(a, b):
    return dot3s(*split(a), *split(b))


def both_layers(*refs):
    refs = list(refs)

    def take(n):
        got = refs[:n]
        del refs[:n]
        return got

    tile_src, tile_row, read_block, degree, raw, adj_hbm, diag_hbm, w1, b1, w2, b2, out_hbm = take(12)
    zflat = take(2 * 2 * NEAR)
    zbuf = [[[zflat[(h * 2 + way) * NEAR + d] for d in range(NEAR)] for way in range(2)] for h in range(2)]
    inc = take(2)
    sendbuf, prod, runs, adjhi, adjlo = take(5)
    agg = take(2)
    vertflat = take(4)
    vert = [vertflat[:2], vertflat[2:]]
    wgflat = take(4)
    wg = [wgflat[:2], wgflat[2:]]
    total, hid = take(2)
    featflat = take(4)
    feats = [featflat[:2], featflat[2:]]
    scal, tblv, tbls, rbrow, tabv, tab, out, verthi, vertlo, diag = take(10)
    weights = [w1, w2]
    biases = [b1, b2]
    sem_tsend, sem_trecv, sem_tloc, sem_zsend, sem_zrecv, sem_xsend, sem_xrecv = take(7)
    sem_wsend, sem_wrecv, sem_wloc, sem_ysend, sem_yrecv, sem_bsend, sem_brecv, sem_adj, sem_tab, sem_out, sem_diag, free = take(12)

    me = lax.axis_index("dom")
    y = lax.axis_index("feat")
    z = me // PLANE
    xc = lax.rem(me, PLANE)
    x = xc // NC
    c = lax.rem(xc, NC)

    def plane(step):
        return lax.rem(z + (step + NZ), NZ) * PLANE

    def seat(dx, dc):
        return lax.rem(x + dx, NX) * NC + lax.rem(c + dc, NC)

    def ypeer(step):
        return lax.rem(y + step, NY)

    def rdma(src, dst, send, recv, device):
        return pltpu.make_async_remote_copy(
            src_ref=src, dst_ref=dst, send_sem=send, recv_sem=recv, device_id=device, device_id_type=MESH
        )

    def signal(sem, device):
        pl.semaphore_signal(sem, inc=1, device_id=device, device_id_type=MESH)

    def signal_writers(sem):
        for dx, dc in READERS:
            signal(sem, (plane(0) + seat(dx, dc), y))
        beyond = lax.rem(z + (4 * c - 2 + NZ), NZ) * PLANE
        for j in range(PLANE):
            signal(sem, (plane(1) + j, y))
            signal(sem, (plane(-1) + j, y))
            signal(sem, (beyond + j, y))

    writers = NREAD + 3 * PLANE

    adj_copy = pltpu.make_async_copy(adj_hbm, prod, sem_adj)
    adj_copy.start()
    diag_copy = pltpu.make_async_copy(diag_hbm, diag, sem_diag)
    diag_copy.start()
    own_weights = []
    for l in range(2):
        for h in range(2):
            own_weights.append(
                pltpu.make_async_copy(
                    weights[l].at[pl.ds(h * HALF, HALF)],
                    wg[l][h].at[pl.ds(pl.multiple_of(y * HALF, HALF), HALF)],
                    sem_wloc.at[l, h],
                )
            )
    for copy in own_weights:
        copy.start()

    rbrow[...] = jnp.zeros((8, TILE), jnp.int32)
    rbrow[0:1, 0:NPARTS] = read_block[...]
    barrier = pltpu.get_barrier_semaphore()
    for dz in TABLE_STEPS[1:-1]:
        signal(barrier, (plane(dz) + xc, y))
    for dy in range(1, NY):
        signal(barrier, (me, ypeer(dy)))
    signal_writers(barrier)

    def scale(i, carry):
        row = lax.rsqrt(degree[pl.ds(i, 1), :].astype(F32))
        scal[i] = jnp.transpose(jnp.broadcast_to(row, (TILE, TILE)))
        factor = scal[i]
        for h in range(2):
            feats[0][h][i] = raw[i, :, h * HALF : (h + 1) * HALF] * factor
        return carry

    lax.fori_loop(0, BLK, scale, 0)
    pl.semaphore_wait(barrier, len(TABLE_STEPS) - 2 + NY - 1 + writers)

    table_copies = {
        dz: rdma(rbrow, tblv.at[dz], sem_tsend.at[dz], sem_trecv.at[dz], (plane(dz) + xc, y)) for dz in TABLE_STEPS
    }

    own_table = pltpu.make_async_copy(rbrow, tbls.at[0], sem_tloc.at[0])
    own_table.start()

    def wait_table(dz):
        table_copies[dz].wait_recv()
        copy = pltpu.make_async_copy(tblv.at[dz], tbls.at[dz], sem_tloc.at[dz])
        copy.start()
        copy.wait()

    def sort_tiles():
        lane = lax.broadcasted_iota(jnp.int32, (TILE, TILE), 1)
        sublane = lax.broadcasted_iota(jnp.int32, (TILE, TILE), 0)
        tabv[...] = jnp.full((8, TILE), BLK + 1, jnp.int32)
        tabv[0:1, 0:REMOTE] = tile_row[...]
        rows = jnp.broadcast_to(tabv[0:1, :], (TILE, TILE))
        rows_down = jnp.transpose(rows)
        key, key_down = rows * TILE + lane, rows_down * TILE + sublane

        def total_of(mask, what):
            return jnp.sum(jnp.where(mask, what, 0), axis=0, keepdims=True)

        rank = total_of(key_down < key, jnp.ones_like(key))
        rank_down = jnp.transpose(jnp.broadcast_to(rank, (TILE, TILE)))
        perm = total_of(rank_down == lane, sublane)
        row = total_of(rank_down == lane, rows_down)
        before = total_of(rank_down == lane - 1, rows_down)
        upto = total_of(rows_down <= lane, jnp.ones_like(key))
        here = total_of(rows_down == lane, jnp.ones_like(key))
        tabv[0:1, :] = perm
        tabv[1:2, :] = jnp.where((row == before) & (lane[0:1] > 0), 1, 0)
        tabv[2:3, :] = jnp.where(here > 0, upto - 1, REMOTE)
        copy = pltpu.make_async_copy(tabv, tab, sem_tab)
        copy.start()
        copy.wait()

    def weight_copy(l, h, dy):
        return rdma(
            weights[l].at[pl.ds(h * HALF, HALF)],
            wg[l][h].at[pl.ds(pl.multiple_of(y * HALF, HALF), HALF)],
            sem_wsend.at[l, h, dy - 1],
            sem_wrecv.at[l, h, dy - 1],
            (me, ypeer(dy)),
        )

    def columns(n):
        return pl.ds(pl.multiple_of(n * FEAT, FEAT), FEAT)

    def zcopy(l, h, way, d, part=None):
        src = feats[l][h] if d == 1 else zbuf[h][way][d - 2]
        dst = zbuf[h][way][d - 1]
        if part is not None:
            blocks = pl.ds(ypeer(part) * MINE, MINE)
            src, dst = src.at[blocks], dst.at[blocks]
        return rdma(
            src,
            dst,
            sem_zsend.at[h, way, d - 1],
            sem_zrecv.at[h, way, d - 1],
            (plane(1 if way == 0 else -1) + xc, y),
        )

    def start_own(l, h, part=None):
        for way in range(2):
            zcopy(l, h, way, 1, part).start()

    def run_layer(l):
        feat = feats[l]

        position = [0, 0]

        def serve(h, dz, ref, far=0):
            slot = plane(dz) + xc
            entry = (-dz) % NZ
            targets = []
            if far:
                targets = [plane(far) + seat(dx, dc) for dx, dc in READERS + [(0, 0)]]
                targets += [plane(2 * far) + lax.rem(x + dx, NX) * NC + (0 if far > 0 else 1) for dx in range(NX)]
            targets += [plane(0) + seat(dx, dc) for dx, dc in READERS]
            base = h * SENDS + position[h]
            position[h] += len(targets)
            for r, target in enumerate(targets):
                sendbuf[base + r] = ref[jnp.minimum(tbls[entry, 0, target], BLK - 1)]
            for r, target in enumerate(targets):
                rdma(
                    sendbuf.at[base + r],
                    inc[h].at[slot],
                    sem_xsend.at[h],
                    sem_xrecv.at[h],
                    (target, y),
                ).start()
            inc[h][slot] = ref[jnp.minimum(tbls[entry, 0, me], BLK - 1)]

        def distance(h, d):
            for way in range(2):
                zcopy(l, h, way, d).wait_recv()
                if d < NEAR:
                    zcopy(l, h, way, d + 1).start()
            for way in range(2):
                dz = -d if way == 0 else d
                if l == 0 and h == 0:
                    wait_table(-dz % NZ)
                serve(h, dz, zbuf[h][way][d - 1], (1 if way == 0 else -1) if d == NEAR else 0)

        def ycopy(h, dy):
            n = ypeer(dy)
            return rdma(
                agg[h].at[pl.ds(pl.multiple_of(n * ROWS, ROWS), ROWS)],
                vert[l][h].at[:, pl.ds(pl.multiple_of(y * HALF, HALF), HALF)],
                sem_ysend.at[h, dy - 1],
                sem_yrecv.at[h, dy - 1],
                (me, n),
            )

        def own_tiles(h):
            def step(i, carry):
                agg[h][pl.ds(pl.multiple_of(i * TILE, TILE), TILE), :] = dot3(
                    diag[i], feat[h][i]
                )
                return carry

            lax.fori_loop(0, BLK, step, 0, unroll=2)

        def aggregate(h):
            many = inc[h].at[pl.ds(0, ARRIVALS)]
            pltpu.make_async_copy(many, many, sem_xrecv.at[h]).wait()

            def group(g, carry):
                block_hi, block_lo = split(inc[h][tile_src[0, 2 * g]])
                pair = dot3s(adjhi[g], adjlo[g], block_hi, block_lo)
                prod[2 * g] = pair[:TILE]
                prod[2 * g + 1] = pair[TILE:]
                return carry

            lax.fori_loop(0, GROUPS, group, 0, unroll=8)

            def run(p, acc):
                acc = acc * tab[1, p].astype(F32) + prod[tab[0, p]]
                runs[p] = acc
                return acc

            lax.fori_loop(0, REMOTE, run, jnp.zeros((TILE, HALF), F32), unroll=8)
            for dy in (1, 2, 3, 0):
                n = ypeer(dy)
                for j in range(MINE):
                    i = n * MINE + j
                    rows = pl.ds(pl.multiple_of(i * TILE, TILE), TILE)
                    value = (agg[h][rows, :] + runs[tab[2, i]]) * scal[i]
                    if dy:
                        agg[h][rows, :] = value
                    else:
                        vert[l][h][j * TILE : (j + 1) * TILE, pl.ds(pl.multiple_of(y * HALF, HALF), HALF)] = value
                if dy:
                    ycopy(h, dy).start()

        def wait_inputs(h):
            own_weights[l * 2 + h].wait()
            for dy in range(1, NY):
                weight_copy(l, h, dy).wait_recv()
            for dy in range(1, NY):
                ycopy(h, dy).wait_recv()

        def load_inputs(h):
            wait_inputs(h)
            hi, lo = split(vert[l][h][...])
            verthi[...] = hi
            vertlo[...] = lo

        def product(h, n):
            return dot3s(verthi[...], vertlo[...], *split(wg[l][h][:, columns(n)]))

        def first_product():
            load_inputs(0)

            def step(n, carry):
                total[n] = product(0, n) + biases[l][:, columns(n)]
                return carry

            lax.fori_loop(0, NY, step, 0)

        def value(n):
            return total[n] + product(1, n)

        def write(n):
            return pltpu.make_async_copy(out.at[:, columns(n)], out_hbm.at[:, columns(n)], sem_out.at[n])

        def last_product():
            load_inputs(1)

            def step(n, carry):
                out[:, columns(n)] = value(n)
                write(n).start()
                return carry

            lax.fori_loop(0, NY, step, 0)
            for n in range(NY):
                write(n).wait()

        def hidden_product():
            load_inputs(1)
            factor = scal[pl.ds(y * MINE, MINE)]

            def hidden(n):
                found = jnp.maximum(value(n), 0.0).reshape(MINE, TILE, FEAT)
                return found * jnp.concatenate([factor, factor], axis=2)

            def step(k, carry):
                n = ypeer(k + 1)
                hid[n] = hidden(n)
                back(0, k).start()
                return carry

            mine = hidden(y)
            for h in range(2):
                feats[1][h][pl.ds(y * MINE, MINE)] = mine[:, :, h * HALF : (h + 1) * HALF]
            lax.fori_loop(0, 1, step, 0)
            pl.semaphore_wait(free, writers)
            for h in range(2):
                start_own(1, h, 0)
            lax.fori_loop(1, NY - 1, step, 0)
            for k in range(NY - 1):
                back(1, k).start()

        def finish_sends():
            for h in range(2):
                for way in range(2):
                    for d in range(1, NEAR + 1):
                        zcopy(l, h, way, d).wait_send()
                many = sendbuf.at[pl.ds(h * SENDS, SENDS)]
                pltpu.make_async_copy(many, many, sem_xsend.at[h]).wait()

        def finish_exchange():
            for h in range(2):
                for dy in range(1, NY):
                    ycopy(h, dy).wait_send()
                    weight_copy(l, h, dy).wait_send()

        if l == 0:
            for h in range(2):
                start_own(l, h)
            for copy in table_copies.values():
                copy.start()
            for ll in range(2):
                for h in range(2):
                    for dy in range(1, NY):
                        weight_copy(ll, h, dy).start()
            own_table.wait()
            for h in range(2):
                serve(h, 0, feat[h])
        else:
            for h in range(2):
                for k in range(NY - 1):
                    back(h, k).wait()
                    start_own(l, h, NY - 1 - k)
                serve(h, 0, feat[h])
        if l == 0:
            adj_copy.wait()
            diag_copy.wait()

            def presplit(g, carry):
                for t in range(2):
                    hi, lo = split(prod[2 * g + t])
                    adjhi[g, t * TILE : (t + 1) * TILE, :] = hi
                    adjlo[g, t * TILE : (t + 1) * TILE, :] = lo
                return carry

            lax.fori_loop(0, GROUPS, presplit, 0)
            runs[REMOTE] = jnp.zeros((TILE, HALF), F32)
        own_tiles(0)
        if l == 0:
            sort_tiles()
        distance(0, 1)
        distance(1, 1)
        own_tiles(1)
        distance(0, 2)
        distance(1, 2)
        aggregate(0)
        first_product()
        aggregate(1)
        finish_sends()
        if l == 0:
            signal_writers(free)
            hidden_product()
        else:
            last_product()
        finish_exchange()

    def back(h, k):
        n = ypeer(k + 1)
        cols = pl.ds(h * HALF, HALF)
        return rdma(
            hid.at[n, :, :, cols],
            feats[1][h].at[pl.ds(y * MINE, MINE)],
            sem_bsend.at[h, k],
            sem_brecv.at[h, k],
            (me, n),
        )

    run_layer(0)
    run_layer(1)
    for copy in table_copies.values():
        copy.wait_send()


def network(*operands):
    vmem = pl.BlockSpec(memory_space=pltpu.VMEM)
    smem = pl.BlockSpec(memory_space=pltpu.SMEM)
    anyw = pl.BlockSpec(memory_space=pl.ANY)
    dma = pltpu.SemaphoreType.DMA
    return pl.pallas_call(
        both_layers,
        name="both_layers",
        out_shape=jax.ShapeDtypeStruct((ROWS, NY * FEAT), F32),
        in_specs=[smem, vmem, vmem, vmem, vmem, anyw, anyw, anyw, vmem, anyw, vmem],
        out_specs=anyw,
        scratch_shapes=[pltpu.VMEM((BLK, TILE, HALF), F32)] * (2 * 2 * NEAR)
        + [pltpu.VMEM((NPARTS, TILE, HALF), F32)] * 2
        + [
            pltpu.VMEM((2 * SENDS, TILE, HALF), F32),
            pltpu.VMEM((REMOTE, TILE, HALF), F32),
            pltpu.VMEM((REMOTE + 1, TILE, HALF), F32),
            pltpu.VMEM((GROUPS, 2 * TILE, TILE), BF16),
            pltpu.VMEM((GROUPS, 2 * TILE, TILE), BF16),
        ]
        + [pltpu.VMEM((NY * ROWS, HALF), F32)] * 2
        + [pltpu.VMEM((ROWS, NY * HALF), F32)] * 4
        + [pltpu.VMEM((NY * HALF, NY * FEAT), F32)] * 4
        + [
            pltpu.VMEM((NY, ROWS, FEAT), F32),
            pltpu.VMEM((NY, MINE, TILE, FEAT), F32),
        ]
        + [pltpu.VMEM((BLK, TILE, HALF), F32)] * 4
        + [
            pltpu.VMEM((BLK, TILE, TILE), F32),
            pltpu.VMEM((NZ, 8, 128), jnp.int32),
            pltpu.SMEM((NZ, 8, 128), jnp.int32),
            pltpu.VMEM((8, TILE), jnp.int32),
            pltpu.VMEM((8, TILE), jnp.int32),
            pltpu.SMEM((8, TILE), jnp.int32),
            pltpu.VMEM((ROWS, NY * FEAT), F32),
            pltpu.VMEM((ROWS, NY * HALF), BF16),
            pltpu.VMEM((ROWS, NY * HALF), BF16),
            pltpu.VMEM((BLK, TILE, TILE), F32),
            dma((NZ,)),
            dma((NZ,)),
            dma((NZ,)),
            dma((2, 2, NEAR)),
            dma((2, 2, NEAR)),
            dma((2,)),
            dma((2,)),
            dma((2, 2, 3)),
            dma((2, 2, 3)),
            dma((2, 2)),
            dma((2, 3)),
            dma((2, 3)),
            dma((2, 3)),
            dma((2, 3)),
            dma,
            dma,
            dma((NY,)),
            dma,
            pltpu.SemaphoreType.REGULAR,
        ],
        compiler_params=pltpu.CompilerParams(
            collective_id=0, has_side_effects=True, vmem_limit_bytes=67_000_000
        ),
    )(*operands)


def per_device(
    features, degree, diag_adj, remote_adj, read_block, tile_src, tile_row, w_first, b_first, w_second, b_second
):
    return network(
        tile_src,
        tile_row,
        read_block,
        degree.reshape(BLK, TILE),
        features.reshape(BLK, TILE, FEAT),
        remote_adj[0],
        diag_adj.reshape(BLK, TILE, TILE),
        w_first,
        b_first[None, :],
        w_second,
        b_second[None, :],
    )


def solution(mesh):
    return jax.shard_map(
        per_device,
        mesh=mesh,
        in_specs=(
            P("dom", "feat"),
            P("dom"),
            P("dom", None),
            P("dom", None, None, None),
            P("dom", None),
            P("dom", None),
            P("dom", None),
            P("feat", None),
            P(),
            P("feat", None),
            P(),
        ),
        out_specs=P(("dom", "feat"), None),
        check_vma=False,
    )
```
